512 devices in a mesh: grid: 32 (over y_lo, z, core), occ: 16 (over x, y_hi).
Axes of the slice: x: 4, y: 8 (y_hi: 4, y_lo: 2; y = y_hi * 2 + y_lo), z: 8, core: 2. Of those that a mesh axis runs over, the one named last changes fastest.
Arguments:
- orbital_values: bfloat16 [8192, 16000], P('grid', 'occ'), may hold values from -6 to 6
- occupied: bfloat16 [16000, 512], P('occ', 'grid'), may hold values from -0.046875 to 0.046875
- trial: bfloat16 [16000, 512], P('occ', 'grid'), may hold values from -0.046875 to 0.046875
- point_weights: float32 [8192], P('grid'), may hold values from 0.1 to 1
- batch_sizes: int32 [256], P('grid'), may hold values from 1 to 32, 4096 in all
- significant: int32 [256, 128], P('grid', 'occ'), may hold values 0 or 1
Outputs:
- exchange: float32 [16000, 512], P('occ', 'grid')
The draws below stay inside these ranges and needn't reach their ends.
Inputs may be any that keep to these rules, and one draw needn't show every extreme that they name: `batch_sizes`: batch sizes sum to 4096 and the largest is exactly 32.
All inputs are finite; a program needn't handle non-finite values. No bound on the sum of `batch_sizes` or of `significant` on one device may be relied on, other than what follows from the above.
Results may differ from the reference program's by a relative error of at most 0.0027.
Values may be sent and summed in bfloat16 or wider, within the bound.
A program may use at most 64 MiB of HBM per device.

```python
import math
import jax
import jax.numpy as jnp
import numpy as np
from jax import lax

NB = 16000
NOCC = 512
NBLOCK = 128
BCAP = 32
NBATCH = 256
NG = 8192


def plant(entries, stream_key, low, top_value):
    index_at = [jax.random.randint(jax.random.fold_in(stream_key, axis), (), 0, length) for axis, length in enumerate(entries.shape)]
    widest = entries.shape.index(max(entries.shape))
    beside = index_at[:widest] + [(index_at[widest] + 1) % entries.shape[widest]] + index_at[widest + 1:]
    return entries.at[tuple(index_at)].set(low).at[tuple(beside)].set(top_value)


def block_scale(rng, extent, pieces, smallest, top_value):
    loudness, own = 1.0, jax.random.fold_in(rng, 6)
    for dim, shards_of in pieces:
        steps = jnp.exp(jax.random.uniform(jax.random.fold_in(own, dim), (shards_of,), jnp.float32, smallest / len(pieces), top_value / len(pieces)))
        loudness = loudness * jnp.repeat(steps, extent[dim] // shards_of).reshape([-1 if axis == dim else 1 for axis in range(len(extent))])
    return loudness


def length_profile(number_of, total, reach, skew):
    weights = [(1 << 20) // math.isqrt(standing ** skew) + 1 for standing in range(2, number_of + 1)]
    rest, holding = total - reach - (number_of - 1), [1] * (number_of - 1)
    while rest > 0:
        candidates = [i for i in range(number_of - 1) if holding[i] < reach]
        whole, remaining = sum([weights[i] for i in candidates]), rest
        for i in candidates:
            addition = min(reach - holding[i], max(1, remaining * weights[i] // whole), rest)
            holding[i] = holding[i] + addition
            rest = rest - addition
    return np.array([reach] + holding)


def uneven_parts(stream_key, count, total, bound, lean):
    if count == 2:
        one = jax.random.randint(stream_key, (), max(1, total - bound), min(bound, total - 1) + 1)
        return jnp.stack([one, total - one])
    lengths = jnp.asarray(length_profile(count, total, bound, lean), jnp.int32)
    twos = (count - 1) // 2
    donor, taker = lengths[1:1 + 2 * twos:2], lengths[2:2 + 2 * twos:2]
    margin = jnp.minimum(donor - 1, bound - taker)
    passed = jax.random.randint(jax.random.fold_in(stream_key, 1), (twos,), 0, 1 << 20) % (margin + 1)
    lengths = lengths.at[1:1 + 2 * twos:2].set(donor - passed).at[2:2 + 2 * twos:2].set(taker + passed)
    return lengths[jax.random.permutation(jax.random.fold_in(stream_key, 2), count)]


def noise(rng, dims, spread, reach, split=(), kind=jnp.bfloat16):
    level = block_scale(rng, dims, split, -0.22, 0.18) if split else 1.0
    drawn = jax.random.normal(rng, dims, jnp.float32) * spread * level
    return jnp.minimum(jnp.maximum(drawn, -reach), reach).astype(kind)


def setup_inputs(seed: int = 0) -> dict:
    key_of = jax.random.split(jax.random.key(seed), 7)
    return {
        "orbital_values": noise(key_of[0], (NG, NB), 1.0, 6.0, ((0, 32), (1, 16))),
        "occupied": noise(key_of[1], (NB, NOCC), NB ** -0.5, 0.046875, ((0, 16), (1, 32))),
        "trial": noise(key_of[2], (NB, NOCC), NB ** -0.5, 0.046875, ((0, 16), (1, 32))),
        "point_weights": jnp.clip(jnp.exp(math.log(1.0) - 2.3025851 * jax.random.uniform(key_of[3], (NG,), jnp.float32) ** block_scale(key_of[3], (NG,), ((0, 32),), -0.2, 0.2)), 0.1, 1.0),
        "batch_sizes": uneven_parts(key_of[4], NBATCH, NBATCH * BCAP // 2, BCAP, 2).astype(jnp.int32),
        "significant": plant((jax.random.randint(key_of[5], (NBATCH, NBLOCK), 0, 4) < 3).astype(jnp.int32), jax.random.fold_in(key_of[5], 1), 0, 1),
    }


def screen(values, sizes, significant):
    rows, cols = values.shape
    batches = sizes.shape[0]
    blocks = significant.shape[1]
    blocked = values.reshape(batches, rows // batches, blocks, cols // blocks) * significant.astype(values.dtype)[:, None, :, None]
    position = lax.broadcasted_iota(jnp.int32, (batches, rows // batches), 1)
    live = (position < sizes[:, None]).astype(jnp.float32).reshape(rows)
    return (blocked.reshape(rows, cols), live)

def reference(orbital_values, occupied, trial, point_weights, batch_sizes, significant):
    screened, live = screen(orbital_values, batch_sizes, significant)
    orbitals = jnp.dot(screened, occupied, preferred_element_type=jnp.float32)
    response = jnp.dot(screened, trial, preferred_element_type=jnp.float32)
    density = lax.optimization_barrier(jnp.sum(orbitals * response, axis=1)) / math.sqrt(NOCC)
    kernel = ((point_weights * live)[:, None] * (density[:, None] * orbitals + response)).astype(jnp.bfloat16)
    summed = lax.dot_general(screened, kernel, (((0,), (0,)), ((), ())), preferred_element_type=jnp.float32)
    return summed / math.sqrt(NG)
```

```python
import functools
import math

import jax
import jax.numpy as jnp
from jax import lax
from jax.experimental import pallas as pl
from jax.experimental.pallas import tpu as pltpu
from jax.sharding import PartitionSpec as P

MESH = pl.DeviceIdType.MESH
NX, NYH, NYL, NZ, NC = 4, 4, 2, 8, 2
CAP = 32

SETS = (
    ((0, 0), (1, 0), (0, 1), (0, 7)),
    ((0, 2), (0, 6), (1, 1), (1, 7)),
    ((0, 3), (0, 5), (1, 2), (1, 6)),
    ((0, 4), (1, 3), (1, 5), (1, 4)),
)
WHERE = {slot: (s, i) for s, row in enumerate(SETS) for i, slot in enumerate(row)}


def kernel(
    v_ref, occ_ref, tri_ref, w_ref, sz_ref, sig_ref, out_ref,
    panels, vraw, sigp, smat, prod,
    x1p, x1m, x3p, x3m, a5p, a5m, x5p, x5m,
    turned, yrecv, dens_out, dens_in, kall,
    xsend, xrecv, zsend, zrecv,
    sems, p_sems, c_sems, x_sems, y_sems, k_sems, d_sems,
):
    g, o = lax.axis_index("grid"), lax.axis_index("occ")
    yl, z, c = g // (NZ * NC), (g // NC) % NZ, g % NC
    x, yh = o // NYH, o % NYH
    nrow = occ_ref.shape[0]
    npt = v_ref.shape[1]

    def grid_at(dy, dz, dc):
        return (((yl + dy) % NYL) * NZ + (z + dz) % NZ) * NC + (c + dc) % NC

    def occ_at(dx, dyh):
        return ((x + dx) % NX) * NYH + (yh + dyh) % NYH

    sent = []

    def send(src, dst, recv_sem, dy=0, dz=0, dc=0, dx=0, dyh=0):
        copy = pltpu.make_async_remote_copy(
            src_ref=src, dst_ref=dst, send_sem=sems.at[len(sent)], recv_sem=recv_sem,
            device_id={"grid": grid_at(dy, dz, dc), "occ": occ_at(dx, dyh)}, device_id_type=MESH,
        )
        copy.start()
        sent.append(copy)

    def arrive(dst, recv_sem):
        pltpu.make_async_remote_copy(
            src_ref=dst, dst_ref=dst, send_sem=sems.at[0], recv_sem=recv_sem,
            device_id={"grid": grid_at(0, 0, 1), "occ": o}, device_id_type=MESH,
        ).wait_recv()

    barrier = pltpu.get_barrier_semaphore()
    peers = (
        dict(dc=1), dict(dy=1), dict(dz=1), dict(dz=7), dict(dx=1), dict(dx=3),
        dict(dyh=1), dict(dyh=2), dict(dyh=3),
    )
    for peer in peers:
        pl.semaphore_signal(
            barrier, inc=1,
            device_id={
                "grid": grid_at(peer.get("dy", 0), peer.get("dz", 0), peer.get("dc", 0)),
                "occ": occ_at(peer.get("dx", 0), peer.get("dyh", 0)),
            },
            device_id_type=MESH,
        )
    pl.semaphore_wait(barrier, len(peers))

    def place(slot, t):
        s, i = WHERE[slot]
        return panels.at[s, t, i]

    def p_sem(slot, t):
        s, i = WHERE[slot]
        return p_sems.at[(s * 4 + i) * 2 + t]

    own = (occ_ref, tri_ref)
    for t in range(2):
        send(own[t], place((0, 7), t), p_sem((0, 7), t), dz=1)
        send(own[t], place((0, 1), t), p_sem((0, 1), t), dz=7)
        send(own[t], place((1, 0), t), p_sem((1, 0), t), dy=1)
    send(sig_ref, sigp, c_sems.at[0], dc=1)
    send(v_ref, vraw, c_sems.at[1], dc=1)
    for t in range(2):
        panels[0, t, 0] = own[t][...]

    def got(slot, t):
        arrive(place(slot, t), p_sem(slot, t))

    def relay(slot, t, moves):
        got(slot, t)
        for to, step in moves:
            send(place(slot, t), place(to, t), p_sem(to, t), **step)

    up, down, over = dict(dz=1), dict(dz=7), dict(dy=1)

    nblock, nbatch = sig_ref.shape[1], sig_ref.shape[0]
    width = v_ref.shape[0] // nblock

    def screen(values, significant):
        sig = significant.astype(jnp.float32).astype(jnp.bfloat16)
        eye = (
            lax.broadcasted_iota(jnp.int32, (nblock, nblock), 0)
            == lax.broadcasted_iota(jnp.int32, (nblock, nblock), 1)
        ).astype(jnp.bfloat16)
        flipped = lax.dot_general(
            eye, sig, (((1,), (1,)), ((), ())), preferred_element_type=jnp.float32
        ).astype(jnp.bfloat16)
        spread = (
            lax.broadcasted_iota(jnp.int32, (nbatch, npt), 1) // CAP
            == lax.broadcasted_iota(jnp.int32, (nbatch, npt), 0)
        ).astype(jnp.bfloat16)
        lanes = jnp.dot(flipped, spread, preferred_element_type=jnp.float32).astype(jnp.bfloat16)
        rows = (
            lax.broadcasted_iota(jnp.int32, (v_ref.shape[0], nblock), 0) // width
            == lax.broadcasted_iota(jnp.int32, (v_ref.shape[0], nblock), 1)
        ).astype(jnp.bfloat16)
        mask = jnp.dot(rows, lanes, preferred_element_type=jnp.float32)
        return values * mask.astype(jnp.bfloat16)

    smat[c] = screen(v_ref[...], sig_ref[...])

    for t in range(2):
        relay((1, 0), t, (((1, 7), up), ((1, 1), down)))
        relay((0, 7), t, (((0, 6), up),))
        relay((0, 1), t, (((0, 2), down),))
    arrive(sigp, c_sems.at[0])
    arrive(vraw, c_sems.at[1])
    smat[1 - c] = screen(vraw[...], sigp[...])

    half = nrow * 4

    def multiply(s):
        lhs = panels[s].reshape(2 * half, v_ref.shape[0])
        for k in range(NC):
            res = jnp.dot(lhs, smat[k], preferred_element_type=jnp.float32)
            for h in range(2):
                prod[s, 2 * k + h] = res[:, h * 128 : (h + 1) * 128]

    lo, hi = pl.ds(0, half), pl.ds(half, half)

    def x_first(s):
        across = prod.at[s, (x + 2) % NX]
        send(across.at[lo], x1p.at[s], x_sems.at[s, 0], dx=1)
        send(across.at[hi], x1m.at[s], x_sems.at[s, 1], dx=3)
        send(prod.at[s, (x + 1) % NX].at[hi], x3p.at[s], x_sems.at[s, 2], dx=1)
        send(prod.at[s, (x + 3) % NX].at[lo], x3m.at[s], x_sems.at[s, 3], dx=3)

    def x_second(s):
        arrive(x1p.at[s], x_sems.at[s, 0])
        a5p[s] = x1p[s] + prod[s, (x + 1) % NX, :half]
        send(a5p.at[s], x5p.at[s], x_sems.at[s, 4], dx=1)
        arrive(x1m.at[s], x_sems.at[s, 1])
        a5m[s] = x1m[s] + prod[s, (x + 3) % NX, half:]
        send(a5m.at[s], x5m.at[s], x_sems.at[s, 5], dx=3)

    def x_last(s):
        arrive(x3p.at[s], x_sems.at[s, 2])
        arrive(x3m.at[s], x_sems.at[s, 3])
        arrive(x5p.at[s], x_sems.at[s, 4])
        arrive(x5m.at[s], x_sems.at[s, 5])
        top = prod[s, x, :half] + x3m[s] + x5p[s]
        low = prod[s, x, half:] + x3p[s] + x5m[s]
        both = jnp.concatenate((top, low), axis=0)
        turned[s] = both.T.reshape(NYH, CAP, 2 * half)
        for k in range(1, NYH):
            send(turned.at[s, (yh + k) % NYH], yrecv.at[s, k - 1], y_sems.at[s, k - 1], dyh=k)

    multiply(0)
    x_first(0)
    for t in range(2):
        relay((0, 6), t, (((0, 5), up),))
        relay((0, 2), t, (((0, 3), down),))
        relay((1, 7), t, (((1, 6), up),))
        relay((1, 1), t, (((1, 2), down),))
    x_second(0)
    multiply(1)
    x_first(1)
    for t in range(2):
        relay((0, 5), t, ((((0, 4), up),) if t == 0 else ()) + (((1, 5), over),))
        relay((0, 3), t, ((((0, 4), down),) if t == 1 else ()) + (((1, 3), over),))
    x_last(0)
    x_second(1)
    for t in range(2):
        got((1, 6), t)
        got((1, 2), t)
    multiply(2)
    x_first(2)
    for t in range(2):
        relay((0, 4), t, (((1, 4), over),))
    x_last(1)
    x_second(2)
    for t in range(2):
        got((1, 5), t)
        got((1, 3), t)
        got((1, 4), t)
    multiply(3)
    x_first(3)
    x_last(2)
    x_second(3)
    x_last(3)

    lane = lax.broadcasted_iota(jnp.int32, (CAP, 2 * half), 1)
    units, rolled = [], []
    part = jnp.zeros((CAP, 1), jnp.float32)
    for s in range(4):
        for k in range(1, NYH):
            arrive(yrecv.at[s, k - 1], y_sems.at[s, k - 1])
        unit = turned[s, yh] + yrecv[s, 0] + yrecv[s, 1] + yrecv[s, 2]
        other = pltpu.roll(unit, half, 1)
        units.append(unit)
        rolled.append(other)
        part += jnp.sum(jnp.where(lane < half, unit * other, 0.0), axis=1, keepdims=True)

    batch = o % nbatch
    row_of = lax.broadcasted_iota(jnp.int32, (CAP, npt), 0)
    lane_of = lax.broadcasted_iota(jnp.int32, (CAP, npt), 1)
    weight = jnp.sum(
        jnp.where(lane_of == row_of + batch * CAP, w_ref[...], 0.0), axis=1, keepdims=True
    )
    count = jnp.sum(
        jnp.where(
            lax.broadcasted_iota(jnp.int32, (1, nbatch), 1) == batch,
            sz_ref[...].astype(jnp.float32), 0.0,
        ),
        axis=1, keepdims=True,
    )
    live = lax.broadcasted_iota(jnp.int32, (CAP, 1), 0).astype(jnp.float32) < count
    weight = jnp.where(live, weight, 0.0)
    dens_out[...] = jnp.where(lane < half, part, weight)
    send(dens_out, dens_in, d_sems.at[0], dc=1)
    arrive(dens_in, d_sems.at[0])
    total = 2 * nrow * NYL * NZ
    density = (part + dens_in[:, 0:1]) * (1.0 / math.sqrt(total))
    weight = jnp.where(o // nbatch == c, weight, dens_in[:, half : half + 1])
    for p in range(2):
        a, b = 2 * p, 2 * p + 1
        value = jnp.where(
            lane < half, density * units[a] + rolled[a], density * rolled[b] + units[b]
        )
        kall[o, :, p * 128 : (p + 1) * 128] = (weight * value).astype(jnp.bfloat16)

    def k_from(dx, dyh):
        return kall.at[occ_at(dx, dyh)]

    for k in range(1, NYH):
        send(k_from(0, 0), k_from(0, 0), k_sems.at[(NYH - k) % NYH], dyh=k)
    for k in (0, 1, 3, 2):
        if k:
            arrive(k_from(0, k), k_sems.at[k])
        for d in (1, 3, 2):
            send(k_from(0, k), k_from(0, k), k_sems.at[((NX - d) % NX) * NYH + k], dx=d)
    for d in (1, 3, 2):
        for k in (0, 1, 3, 2):
            arrive(k_from(d, k), k_sems.at[d * NYH + k])

    kt = [
        kall[k * nbatch : (k + 1) * nbatch].reshape(npt, 4 * half).T for k in range(NC)
    ]

    ys = [(dz, WHERE[(1, dz)]) for dz in range(NZ)]
    held = {}
    for s in (3, 2, 1, 0):
        res = sum(
            lax.dot_general(
                kt[k][s * half : (s + 1) * half], smat[k], (((1,), (1,)), ((), ())),
                preferred_element_type=jnp.float32,
            )
            for k in range(NC)
        )
        for i, (dy, dz) in enumerate(SETS[s]):
            block = res[i * nrow : (i + 1) * nrow]
            if dy:
                xsend[dz] = block.astype(jnp.bfloat16)
                send(xsend.at[dz], xrecv.at[dz], d_sems.at[1 + dz], dy=1)
            else:
                held[dz] = block
    mine = None
    for dz in (4, 3, 5, 2, 6, 1, 7, 0):
        arrive(xrecv.at[dz], d_sems.at[1 + dz])
        value = held[dz] + xrecv[dz].astype(jnp.float32)
        if dz:
            zsend[dz - 1] = value.astype(jnp.bfloat16)
            send(zsend.at[dz - 1], zrecv.at[dz - 1], d_sems.at[8 + dz], dz=dz)
        else:
            mine = value
    for dz in (1, 7, 2, 6, 3, 5, 4):
        arrive(zrecv.at[dz - 1], d_sems.at[8 + dz])
        mine = mine + zrecv[dz - 1].astype(jnp.float32)
    points = npt * NYL * NZ * NC
    out_ref[...] = mine * (1.0 / math.sqrt(points))
    for copy in sent:
        copy.wait_send()


def per_device(orbital_values, occupied, trial, point_weights, batch_sizes, significant):
    v, occ, tri = orbital_values.T, occupied.T, trial.T
    m, npt = v.shape
    nrow = occ.shape[0]
    half = 4 * nrow
    f32, bf16 = jnp.float32, jnp.bfloat16
    dma = pltpu.SemaphoreType.DMA
    out = pl.pallas_call(
        kernel,
        out_shape=jax.ShapeDtypeStruct((nrow, m), f32),
        in_specs=[pl.BlockSpec(memory_space=pltpu.VMEM)] * 6,
        out_specs=pl.BlockSpec(memory_space=pltpu.VMEM),
        scratch_shapes=[
            pltpu.VMEM((4, 2, 4, nrow, m), bf16),
            pltpu.VMEM((m, npt), bf16),
            pltpu.VMEM(significant.shape, jnp.int32),
            pltpu.VMEM((NC, m, npt), bf16),
            pltpu.VMEM((4, NX, 2 * half, 128), f32),
        ]
        + [pltpu.VMEM((4, half, 128), f32)] * 8
        + [
            pltpu.VMEM((4, NYH, CAP, 2 * half), f32),
            pltpu.VMEM((4, NYH - 1, CAP, 2 * half), f32),
            pltpu.VMEM((CAP, 2 * half), f32),
            pltpu.VMEM((CAP, 2 * half), f32),
            pltpu.VMEM((NX * NYH, CAP, 4 * half), bf16),
            pltpu.VMEM((NZ, nrow, m), bf16),
            pltpu.VMEM((NZ, nrow, m), bf16),
            pltpu.VMEM((NZ - 1, nrow, m), bf16),
            pltpu.VMEM((NZ - 1, nrow, m), bf16),
            dma((128,)),
            dma((32,)),
            dma((2,)),
            dma((4, 6)),
            dma((4, NYH - 1)),
            dma((NX * NYH,)),
            dma((1 + 8 + 8,)),
        ],
        compiler_params=pltpu.CompilerParams(
            collective_id=0, has_side_effects=True, vmem_limit_bytes=48 << 20
        ),
    )(v, occ, tri, point_weights.reshape(1, -1), batch_sizes.reshape(1, -1), significant)
    return out.T


def solution(mesh):
    placed = (
        P("grid", "occ"),
        P("occ", "grid"),
        P("occ", "grid"),
        P("grid"),
        P("grid"),
        P("grid", "occ"),
    )
    return jax.shard_map(
        per_device, mesh=mesh, in_specs=placed, out_specs=P("occ", "grid"), check_vma=False
    )
```

```python
import functools
import math

import jax
import jax.numpy as jnp
from jax import lax
from jax.experimental import pallas as pl
from jax.experimental.pallas import tpu as pltpu
from jax.sharding import PartitionSpec as P

MESH = pl.DeviceIdType.MESH
NX, NYH, NYL, NZ, NC = 4, 4, 2, 8, 2
CAP = 32

SETS = (
    ((0, 0), (1, 0), (0, 1), (0, 7)),
    ((0, 2), (0, 6), (1, 1), (1, 7)),
    ((0, 3), (0, 5), (0, 4), (1, 2)),
    ((1, 6), (1, 3), (1, 5), (1, 4)),
)
WHERE = {slot: (s, i) for s, row in enumerate(SETS) for i, slot in enumerate(row)}


def kernel(
    v_hbm, occ_hbm, tri_hbm, w_hbm, sz_hbm, sig_hbm, out_ref,
    v_ref, w_ref, sz_ref, sig_ref, panels, vraw, sigp, smat, stran, prod,
    xin,
    turned, yrecv, dens_out, dens_in, kall,
    xsend, xrecv, zsend, zrecv,
    sems, p_sems, c_sems, x_sems, y_sems, k_sems, d_sems, l_sems,
    near, far, ready_x, ready_z, far_z,
):
    g, o = lax.axis_index("grid"), lax.axis_index("occ")
    yl, z, c = g // (NZ * NC), (g // NC) % NZ, g % NC
    x, yh = o // NYH, o % NYH
    nrow = occ_hbm.shape[0]
    npt = v_ref.shape[1]

    def grid_at(dy, dz, dc):
        return (((yl + dy) % NYL) * NZ + (z + dz) % NZ) * NC + (c + dc) % NC

    def occ_at(dx, dyh):
        return ((x + dx) % NX) * NYH + (yh + dyh) % NYH

    sent = []

    def send(src, dst, recv_sem, dy=0, dz=0, dc=0, dx=0, dyh=0):
        copy = pltpu.make_async_remote_copy(
            src_ref=src, dst_ref=dst, send_sem=sems.at[len(sent)], recv_sem=recv_sem,
            device_id=at(dy, dz, dc, dx, dyh), device_id_type=MESH,
        )
        copy.start()
        sent.append(copy)

    def arrive(dst, recv_sem):
        pltpu.make_async_remote_copy(
            src_ref=dst, dst_ref=dst, send_sem=sems.at[0], recv_sem=recv_sem,
            device_id=at(dc=1), device_id_type=MESH,
        ).wait_recv()

    own = (occ_hbm, tri_hbm)
    loads = [
        pltpu.make_async_copy(src, dst, l_sems.at[n])
        for n, (src, dst) in enumerate((
            (sig_hbm, sig_ref), (v_hbm, v_ref), (occ_hbm, panels.at[0, 0, 0]),
            (tri_hbm, panels.at[0, 1, 0]), (w_hbm, w_ref), (sz_hbm, sz_ref),
        ))
    ]
    for load in loads:
        load.start()

    def at(dy=0, dz=0, dc=0, dx=0, dyh=0):
        return {"grid": grid_at(dy, dz, dc), "occ": occ_at(dx, dyh)}

    def signal(sem, where):
        pl.semaphore_signal(sem, inc=1, device_id=where, device_id_type=MESH)

    beside = (at(dy=1, dyh=yl), at(dy=1, dyh=yl + NYH - 1))
    barrier = pltpu.get_barrier_semaphore()
    peers = (at(dc=1), at(dz=1), at(dz=7), at(dx=1), at(dx=3)) + beside
    for peer in peers:
        signal(barrier, peer)
    pl.semaphore_wait(barrier, len(peers))
    for peer in beside:
        signal(near, peer)
    for peer in (at(dx=1), at(dx=3)):
        signal(ready_x, peer)
    for peer in (at(dz=1), at(dz=7)):
        signal(ready_z, peer)

    def place(slot, t):
        s, i = WHERE[slot]
        return panels.at[s, t, i]

    def p_sem(slot, t):
        s, i = WHERE[slot]
        return p_sems.at[(s * 4 + i) * 2 + t]

    for t in range(2):
        send(own[t], place((0, 7), t), p_sem((0, 7), t), dz=1)
        send(own[t], place((0, 1), t), p_sem((0, 1), t), dz=7)
    for t in range(2):
        send(own[t], place((1, 0), t), p_sem((1, 0), t), dy=1)
    send(sig_hbm, sigp, c_sems.at[0], dc=1)
    send(v_hbm, vraw, c_sems.at[1], dc=1)
    pl.semaphore_wait(ready_z, 2)
    for step in (2, 6):
        signal(far_z, at(dz=step))

    def got(slot, t):
        arrive(place(slot, t), p_sem(slot, t))

    def relay(slot, t, moves):
        got(slot, t)
        for to, step in moves:
            send(place(slot, t), place(to, t), p_sem(to, t), **step)

    up, down, over = dict(dz=1), dict(dz=7), dict(dy=1)

    nblock, nbatch = sig_ref.shape[1], sig_ref.shape[0]
    width = v_ref.shape[0] // nblock

    def screen(values, significant):
        sig = significant.astype(jnp.float32).astype(jnp.bfloat16)
        eye = (
            lax.broadcasted_iota(jnp.int32, (nblock, nblock), 0)
            == lax.broadcasted_iota(jnp.int32, (nblock, nblock), 1)
        ).astype(jnp.bfloat16)
        flipped = lax.dot_general(
            eye, sig, (((1,), (1,)), ((), ())), preferred_element_type=jnp.float32
        ).astype(jnp.bfloat16)
        spread = (
            lax.broadcasted_iota(jnp.int32, (nbatch, npt), 1) // CAP
            == lax.broadcasted_iota(jnp.int32, (nbatch, npt), 0)
        ).astype(jnp.bfloat16)
        lanes = jnp.dot(flipped, spread, preferred_element_type=jnp.float32).astype(jnp.bfloat16)
        rows = (
            lax.broadcasted_iota(jnp.int32, (v_ref.shape[0], nblock), 0) // width
            == lax.broadcasted_iota(jnp.int32, (v_ref.shape[0], nblock), 1)
        ).astype(jnp.bfloat16)
        mask = jnp.dot(rows, lanes, preferred_element_type=jnp.float32)
        return values * mask.astype(jnp.bfloat16)

    for load in loads:
        load.wait()
    smat[c] = screen(v_ref[...], sig_ref[...])
    pl.semaphore_wait(far_z, 2)
    for t in range(2):
        send(own[t], place((0, 4), t), p_sem((0, 4), t), dz=4)

    for t in range(2):
        relay((0, 7), t, (((0, 6), up), ((1, 7), over)))
        relay((0, 1), t, (((0, 2), down), ((1, 1), over)))
    pl.semaphore_wait(near, 2)
    for k in (1, 3):
        signal(far, at(dyh=k))
    arrive(sigp, c_sems.at[0])
    arrive(vraw, c_sems.at[1])
    smat[1 - c] = screen(vraw[...], sigp[...])

    for k in range(NC):
        stran[k] = smat[k].T
    half = nrow * 4

    def multiply(s):
        lhs = panels[s].reshape(2 * half, v_ref.shape[0])
        for k in range(NC):
            res = jnp.dot(lhs, smat[k], preferred_element_type=jnp.float32)
            for h in range(2):
                prod[s, 2 * k + h] = res[:, h * 128 : (h + 1) * 128]

    def x_first(s):
        for d in (2, 1, 3):
            send(prod.at[s, (x + d) % NX], xin.at[s, d - 1], x_sems.at[s, d - 1], dx=d)

    def x_last(s):
        for d in range(1, NX):
            arrive(xin.at[s, d - 1], x_sems.at[s, d - 1])
        both = prod[s, x] + xin[s, 0] + xin[s, 1] + xin[s, 2]
        turned[s] = both.T.reshape(NYH, CAP, 2 * half)
        for k in (2, 1, 3):
            send(turned.at[s, (yh + k) % NYH], yrecv.at[s, k - 1], y_sems.at[s, k - 1], dyh=k)

    for t in range(2):
        got((1, 0), t)
    pl.semaphore_wait(ready_x, 2)
    multiply(0)
    x_first(0)
    for t in range(2):
        relay((0, 6), t, (((0, 5), up),))
        relay((0, 2), t, (((0, 3), down),))
    for t in range(2):
        relay((1, 7), t, (((1, 6), up),))
        relay((1, 1), t, (((1, 2), down),))
    multiply(1)
    x_first(1)
    pl.semaphore_wait(far, 2)
    for t in range(2):
        relay((0, 4), t, (((1, 4), over),))
    for t in range(2):
        relay((0, 5), t, (((1, 5), over),))
        relay((0, 3), t, (((1, 3), over),))
    for t in range(2):
        got((1, 2), t)
    multiply(2)
    x_first(2)
    x_last(0)
    for t in range(2):
        got((1, 6), t)
        got((1, 4), t)
        got((1, 5), t)
        got((1, 3), t)
    multiply(3)
    x_first(3)
    x_last(1)
    x_last(2)
    x_last(3)

    lane = lax.broadcasted_iota(jnp.int32, (CAP, 2 * half), 1)
    units, rolled = [], []
    part = jnp.zeros((CAP, 1), jnp.float32)
    for s in range(4):
        for k in range(1, NYH):
            arrive(yrecv.at[s, k - 1], y_sems.at[s, k - 1])
        unit = turned[s, yh] + yrecv[s, 0] + yrecv[s, 1] + yrecv[s, 2]
        other = pltpu.roll(unit, half, 1)
        units.append(unit)
        rolled.append(other)
        part += jnp.sum(jnp.where(lane < half, unit * other, 0.0), axis=1, keepdims=True)

    batch = o % nbatch
    row_of = lax.broadcasted_iota(jnp.int32, (CAP, npt), 0)
    lane_of = lax.broadcasted_iota(jnp.int32, (CAP, npt), 1)
    weight = jnp.sum(
        jnp.where(lane_of == row_of + batch * CAP, w_ref[...], 0.0), axis=1, keepdims=True
    )
    count = jnp.sum(
        jnp.where(
            lax.broadcasted_iota(jnp.int32, (1, nbatch), 1) == batch,
            sz_ref[...].astype(jnp.float32), 0.0,
        ),
        axis=1, keepdims=True,
    )
    live = lax.broadcasted_iota(jnp.int32, (CAP, 1), 0).astype(jnp.float32) < count
    weight = jnp.where(live, weight, 0.0)
    dens_out[...] = jnp.where(lane < half, part, weight)
    send(dens_out, dens_in, d_sems.at[0], dc=1)
    arrive(dens_in, d_sems.at[0])
    total = 2 * nrow * NYL * NZ
    density = (part + dens_in[:, 0:1]) * (1.0 / math.sqrt(total))
    weight = jnp.where(o // nbatch == c, weight, dens_in[:, half : half + 1])
    for p in range(2):
        a, b = 2 * p, 2 * p + 1
        value = jnp.where(
            lane < half, density * units[a] + rolled[a], density * rolled[b] + units[b]
        )
        kall[p, o] = (weight * value).astype(jnp.bfloat16)

    def k_from(p, dx, dyh):
        return kall.at[p, occ_at(dx, dyh)]

    for p in (1, 0):
        for k in (2, 1, 3):
            send(k_from(p, 0, 0), k_from(p, 0, 0), k_sems.at[p, 0, NYH - k], dyh=k)
    for p in (1, 0):
        for k in (0, 1, 3, 2):
            if k:
                arrive(k_from(p, 0, k), k_sems.at[p, 0, k])
            for d in (2, 1, 3):
                send(k_from(p, 0, k), k_from(p, 0, k), k_sems.at[p, NX - d, k], dx=d)
    held = {}
    for p in (1, 0):
        for k in (0, 1, 3, 2):
            for d in (1, 3, 2):
                arrive(k_from(p, d, k), k_sems.at[p, d, k])
        kt = kall[p].reshape(2 * npt, 2 * half).T
        res = sum(
            jnp.dot(
                kt[:, k * npt : (k + 1) * npt], stran[k], preferred_element_type=jnp.float32
            )
            for k in range(NC)
        )
        slots = SETS[2 * p] + SETS[2 * p + 1]
        for dz in (4, 3, 5, 2, 6, 1, 7, 0):
            for dy in (1, 0):
                if (dy, dz) in slots:
                    i = slots.index((dy, dz))
                    block = res[i * nrow : (i + 1) * nrow]
                    if dy:
                        xsend[dz] = block.astype(jnp.bfloat16)
                        send(xsend.at[dz], xrecv.at[dz], d_sems.at[1 + dz], dy=1)
                    else:
                        held[dz] = block
    mine = None
    for dz in (4, 3, 5, 2, 6, 1, 7, 0):
        arrive(xrecv.at[dz], d_sems.at[1 + dz])
        value = held[dz] + xrecv[dz].astype(jnp.float32)
        if dz:
            zsend[dz - 1] = value.astype(jnp.bfloat16)
            send(zsend.at[dz - 1], zrecv.at[dz - 1], d_sems.at[8 + dz], dz=dz)
        else:
            mine = value
    for dz in (1, 7, 2, 6, 3, 5, 4):
        arrive(zrecv.at[dz - 1], d_sems.at[8 + dz])
        mine = mine + zrecv[dz - 1].astype(jnp.float32)
    points = npt * NYL * NZ * NC
    out_ref[...] = mine * (1.0 / math.sqrt(points))
    for copy in sent:
        copy.wait_send()


def per_device(orbital_values, occupied, trial, point_weights, batch_sizes, significant):
    v, occ, tri = orbital_values.T, occupied.T, trial.T
    m, npt = v.shape
    nrow = occ.shape[0]
    half = 4 * nrow
    f32, bf16 = jnp.float32, jnp.bfloat16
    dma = pltpu.SemaphoreType.DMA
    out = pl.pallas_call(
        kernel,
        out_shape=jax.ShapeDtypeStruct((nrow, m), f32),
        in_specs=[pl.BlockSpec(memory_space=pl.ANY)] * 6,
        out_specs=pl.BlockSpec(memory_space=pltpu.VMEM),
        scratch_shapes=[
            pltpu.VMEM((m, npt), bf16),
            pltpu.VMEM((1, npt), f32),
            pltpu.VMEM((1, batch_sizes.shape[0]), jnp.int32),
            pltpu.VMEM(significant.shape, jnp.int32),
            pltpu.VMEM((4, 2, 4, nrow, m), bf16),
            pltpu.VMEM((m, npt), bf16),
            pltpu.VMEM(significant.shape, jnp.int32),
            pltpu.VMEM((NC, m, npt), bf16),
            pltpu.VMEM((NC, npt, m), bf16),
            pltpu.VMEM((4, NX, 2 * half, 128), f32),
        ]
        + [
            pltpu.VMEM((4, NX - 1, 2 * half, 128), f32),
            pltpu.VMEM((4, NYH, CAP, 2 * half), f32),
            pltpu.VMEM((4, NYH - 1, CAP, 2 * half), f32),
            pltpu.VMEM((CAP, 2 * half), f32),
            pltpu.VMEM((CAP, 2 * half), f32),
            pltpu.VMEM((2, NX * NYH, CAP, 2 * half), bf16),
            pltpu.VMEM((NZ, nrow, m), bf16),
            pltpu.VMEM((NZ, nrow, m), bf16),
            pltpu.VMEM((NZ - 1, nrow, m), bf16),
            pltpu.VMEM((NZ - 1, nrow, m), bf16),
            dma((160,)),
            dma((32,)),
            dma((2,)),
            dma((4, NX - 1)),
            dma((4, NYH - 1)),
            dma((2, NX, NYH)),
            dma((1 + 8 + 8,)),
            dma((6,)),
        ]
        + [pltpu.SemaphoreType.REGULAR] * 5,
        compiler_params=pltpu.CompilerParams(
            collective_id=0, has_side_effects=True, vmem_limit_bytes=24 << 20
        ),
    )(*(
        pltpu.with_memory_space_constraint(a, pltpu.HBM)
        for a in (v, occ, tri, point_weights.reshape(1, -1), batch_sizes.reshape(1, -1), significant)
    ))
    return out.T


def solution(mesh):
    placed = (
        P("grid", "occ"),
        P("occ", "grid"),
        P("occ", "grid"),
        P("grid"),
        P("grid"),
        P("grid", "occ"),
    )
    return jax.shard_map(
        per_device, mesh=mesh, in_specs=placed, out_specs=P("occ", "grid"), check_vma=False
    )
```

```python
import functools
import math

import jax
import jax.numpy as jnp
from jax import lax
from jax.experimental import pallas as pl
from jax.experimental.pallas import tpu as pltpu
from jax.sharding import PartitionSpec as P

MESH = pl.DeviceIdType.MESH
NX, NYH, NYL, NZ, NC = 4, 4, 2, 8, 2
CAP = 32

SETS = (
    ((0, 0), (1, 0), (0, 1), (0, 7)),
    ((0, 2), (0, 6), (1, 1), (1, 7)),
    ((0, 4), (0, 3), (1, 2), (1, 6)),
    ((0, 5), (1, 4), (1, 3), (1, 5)),
)
WHERE = {slot: (s, i) for s, row in enumerate(SETS) for i, slot in enumerate(row)}


def kernel(
    v_hbm, occ_hbm, tri_hbm, w_hbm, sz_hbm, sig_hbm, out_ref,
    v_ref, w_ref, sz_ref, sig_ref, mine_ref, panels, vraw, sigp, smat, stran, prod,
    xin,
    turned, yrecv, dens_out, dens_in, kall,
    xsend, xrecv, zsend, zrecv,
    sems, p_sems, c_sems, x_sems, y_sems, k_sems, d_sems, l_sems,
    near, far, ready_x, ready_z, far_z,
):
    g, o = lax.axis_index("grid"), lax.axis_index("occ")
    yl, z, c = g // (NZ * NC), (g // NC) % NZ, g % NC
    x, yh = o // NYH, o % NYH
    nrow = occ_hbm.shape[0]
    npt = v_ref.shape[1]

    def grid_at(dy, dz, dc):
        return (((yl + dy) % NYL) * NZ + (z + dz) % NZ) * NC + (c + dc) % NC

    def occ_at(dx, dyh):
        return ((x + dx) % NX) * NYH + (yh + dyh) % NYH

    sent = []

    def send(src, dst, recv_sem, dy=0, dz=0, dc=0, dx=0, dyh=0):
        copy = pltpu.make_async_remote_copy(
            src_ref=src, dst_ref=dst, send_sem=sems.at[len(sent)], recv_sem=recv_sem,
            device_id=at(dy, dz, dc, dx, dyh), device_id_type=MESH,
        )
        copy.start()
        sent.append(copy)

    def arrive(dst, recv_sem):
        pltpu.make_async_remote_copy(
            src_ref=dst, dst_ref=dst, send_sem=sems.at[0], recv_sem=recv_sem,
            device_id=at(dc=1), device_id_type=MESH,
        ).wait_recv()

    m, wide = v_hbm.shape[0], panels.shape[-1]
    loads = [
        pltpu.make_async_copy(src, dst, l_sems.at[n])
        for n, (src, dst) in enumerate((
            (occ_hbm, mine_ref.at[0]), (tri_hbm, mine_ref.at[1]), (sig_hbm, sig_ref),
            (v_hbm, v_ref), (w_hbm, w_ref), (sz_hbm, sz_ref),
        ))
    ]
    for load in loads:
        load.start()
    smat[:, m:] = jnp.zeros((NC, wide - m, npt), smat.dtype)

    def at(dy=0, dz=0, dc=0, dx=0, dyh=0):
        return {"grid": grid_at(dy, dz, dc), "occ": occ_at(dx, dyh)}

    def signal(sem, where):
        pl.semaphore_signal(sem, inc=1, device_id=where, device_id_type=MESH)

    beside = (at(dy=1, dyh=yl), at(dy=1, dyh=yl + NYH - 1))
    barrier = pltpu.get_barrier_semaphore()
    peers = (at(dc=1), at(dz=1), at(dz=7), at(dx=1), at(dx=3)) + beside
    for peer in peers:
        signal(barrier, peer)
    for load in loads:
        load.wait()
    panels[0, :, 0, :, :m] = mine_ref[...]
    panels[0, :, 0, :, m:] = jnp.zeros((2, nrow, wide - m), panels.dtype)
    pl.semaphore_wait(barrier, len(peers))
    for peer in beside:
        signal(near, peer)
    for peer in (at(dx=1), at(dx=3)):
        signal(ready_x, peer)
    for peer in (at(dz=1), at(dz=7)):
        signal(ready_z, peer)

    def place(slot, q):
        s, i = WHERE[slot]
        return panels.at[s, q // 2, i, :, pl.ds((q % 2) * (wide // 2), wide // 2)]

    def p_sem(slot, q):
        s, i = WHERE[slot]
        return p_sems.at[(s * 4 + i) * 4 + q]

    for q in range(4):
        send(place((0, 0), q), place((0, 7), q), p_sem((0, 7), q), dz=1)
        send(place((0, 0), q), place((0, 1), q), p_sem((0, 1), q), dz=7)
        send(place((0, 0), q), place((1, 0), q), p_sem((1, 0), q), dy=1)
    send(sig_hbm, sigp, c_sems.at[0], dc=1)
    send(v_hbm, vraw, c_sems.at[1], dc=1)
    pl.semaphore_wait(ready_z, 2)
    for step in (2, 6):
        signal(far_z, at(dz=step))

    def got(*slots):
        for slot in slots:
            for q in range(4):
                arrive(place(slot, q), p_sem(slot, q))

    def relay(slot, q, *moves):
        arrive(place(slot, q), p_sem(slot, q))
        for to, step in moves:
            send(place(slot, q), place(to, q), p_sem(to, q), **step)

    up, down, over = dict(dz=1), dict(dz=7), dict(dy=1)

    nblock, nbatch = sig_ref.shape[1], sig_ref.shape[0]
    width = v_ref.shape[0] // nblock

    def screen(values, significant):
        sig = significant.astype(jnp.float32).astype(jnp.bfloat16)
        eye = (
            lax.broadcasted_iota(jnp.int32, (nblock, nblock), 0)
            == lax.broadcasted_iota(jnp.int32, (nblock, nblock), 1)
        ).astype(jnp.bfloat16)
        flipped = lax.dot_general(
            eye, sig, (((1,), (1,)), ((), ())), preferred_element_type=jnp.float32
        ).astype(jnp.bfloat16)
        spread = (
            lax.broadcasted_iota(jnp.int32, (nbatch, npt), 1) // CAP
            == lax.broadcasted_iota(jnp.int32, (nbatch, npt), 0)
        ).astype(jnp.bfloat16)
        lanes = jnp.dot(flipped, spread, preferred_element_type=jnp.float32).astype(jnp.bfloat16)
        rows = (
            lax.broadcasted_iota(jnp.int32, (v_ref.shape[0], nblock), 0) // width
            == lax.broadcasted_iota(jnp.int32, (v_ref.shape[0], nblock), 1)
        ).astype(jnp.bfloat16)
        mask = jnp.dot(rows, lanes, preferred_element_type=jnp.float32)
        return values * mask.astype(jnp.bfloat16)

    smat[c, :m] = screen(v_ref[...], sig_ref[...])
    pl.semaphore_wait(near, 2)
    for k in (1, 3):
        signal(far, at(dyh=k))
    arrive(sigp, c_sems.at[0])
    arrive(vraw, c_sems.at[1])
    smat[1 - c, :m] = screen(vraw[...], sigp[...])
    pl.semaphore_wait(far_z, 2)
    for q in range(4):
        relay((0, 7), q, ((0, 6), up), ((1, 7), over), *([((0, 4), dict(dz=3))] if q < 2 else []))
        relay((0, 1), q, ((0, 2), down), ((1, 1), over), *([((0, 4), dict(dz=5))] if q > 1 else []))
    for k in range(NC):
        stran[k] = smat[k].T
    half = nrow * 4

    def multiply(s):
        lhs = panels[s].reshape(2 * half, wide)
        for k in range(NC):
            res = jnp.dot(lhs, smat[k], preferred_element_type=jnp.float32)
            for h in range(2):
                prod[s, 2 * k + h] = res[:, h * 128 : (h + 1) * 128]

    def x_first(s):
        for d in (2, 1, 3):
            send(prod.at[s, (x + d) % NX], xin.at[s, d - 1], x_sems.at[s, d - 1], dx=d)

    def x_last(s):
        for d in range(1, NX):
            arrive(xin.at[s, d - 1], x_sems.at[s, d - 1])
        both = prod[s, x] + xin[s, 0] + xin[s, 1] + xin[s, 2]
        turned[s] = both.T.reshape(NYH, CAP, 2 * half)
        for k in (2, 1, 3):
            send(turned.at[s, (yh + k) % NYH], yrecv.at[s, k - 1], y_sems.at[s, k - 1], dyh=k)

    got((1, 0))
    pl.semaphore_wait(ready_x, 2)
    multiply(0)
    x_first(0)
    for q in range(4):
        relay((0, 6), q, ((0, 5), up), ((1, 6), over))
        relay((0, 2), q, ((0, 3), down), ((1, 2), over))
        relay((1, 7), q, ((1, 5), dict(dz=2)))
        relay((1, 1), q, ((1, 3), dict(dz=6)))
    multiply(1)
    x_first(1)
    pl.semaphore_wait(far, 2)
    for q in (2, 0, 1, 3):
        relay((0, 4), q, ((1, 4), over))
    got((1, 2), (1, 6), (0, 3))
    multiply(2)
    x_first(2)
    x_last(0)
    got((0, 5), (1, 4), (1, 5), (1, 3))
    multiply(3)
    x_first(3)
    x_last(1)
    x_last(2)
    x_last(3)

    lane = lax.broadcasted_iota(jnp.int32, (CAP, 2 * half), 1)
    units, rolled = [], []
    part = jnp.zeros((CAP, 1), jnp.float32)
    for s in range(4):
        for k in range(1, NYH):
            arrive(yrecv.at[s, k - 1], y_sems.at[s, k - 1])
        unit = turned[s, yh] + yrecv[s, 0] + yrecv[s, 1] + yrecv[s, 2]
        other = pltpu.roll(unit, half, 1)
        units.append(unit)
        rolled.append(other)
        part += jnp.sum(jnp.where(lane < half, unit * other, 0.0), axis=1, keepdims=True)

    batch = o % nbatch
    row_of = lax.broadcasted_iota(jnp.int32, (CAP, npt), 0)
    lane_of = lax.broadcasted_iota(jnp.int32, (CAP, npt), 1)
    weight = jnp.sum(
        jnp.where(lane_of == row_of + batch * CAP, w_ref[...], 0.0), axis=1, keepdims=True
    )
    count = jnp.sum(
        jnp.where(
            lax.broadcasted_iota(jnp.int32, (1, nbatch), 1) == batch,
            sz_ref[...].astype(jnp.float32), 0.0,
        ),
        axis=1, keepdims=True,
    )
    live = lax.broadcasted_iota(jnp.int32, (CAP, 1), 0).astype(jnp.float32) < count
    weight = jnp.where(live, weight, 0.0)
    dens_out[...] = jnp.where(lane < half, part, weight)
    send(dens_out, dens_in, d_sems.at[0], dc=1)
    arrive(dens_in, d_sems.at[0])
    total = 2 * nrow * NYL * NZ
    density = (part + dens_in[:, 0:1]) * (1.0 / math.sqrt(total))
    weight = jnp.where(o // nbatch == c, weight, dens_in[:, half : half + 1])
    for p in range(2):
        a, b = 2 * p, 2 * p + 1
        value = jnp.where(
            lane < half, density * units[a] + rolled[a], density * rolled[b] + units[b]
        )
        kall[p, o] = (weight * value).astype(jnp.bfloat16)

    def k_from(p, dx, dyh):
        return kall.at[p, occ_at(dx, dyh)]

    for p in (1, 0):
        for k in (2, 1, 3):
            send(k_from(p, 0, 0), k_from(p, 0, 0), k_sems.at[p, 0, NYH - k], dyh=k)
    for p in (1, 0):
        for k in (0, 1, 3, 2):
            if k:
                arrive(k_from(p, 0, k), k_sems.at[p, 0, k])
            for d in (2, 1, 3):
                send(k_from(p, 0, k), k_from(p, 0, k), k_sems.at[p, NX - d, k], dx=d)
    held = {}
    for p in (1, 0):
        for k in (0, 1, 3, 2):
            for d in (1, 3, 2):
                arrive(k_from(p, d, k), k_sems.at[p, d, k])
        kt = kall[p].reshape(2 * npt, 2 * half).T
        res = sum(
            jnp.dot(
                kt[:, k * npt : (k + 1) * npt], stran[k], preferred_element_type=jnp.float32
            )
            for k in range(NC)
        )
        slots = SETS[2 * p] + SETS[2 * p + 1]
        for dz in (4, 3, 5, 2, 6, 1, 7, 0):
            for dy in (1, 0):
                if (dy, dz) in slots:
                    i = slots.index((dy, dz))
                    block = res[i * nrow : (i + 1) * nrow]
                    if dy:
                        xsend[dz] = block.astype(jnp.bfloat16)
                        send(xsend.at[dz], xrecv.at[dz], d_sems.at[1 + dz], dy=1)
                    else:
                        held[dz] = block
    mine = None
    for dz in (4, 3, 5, 2, 6, 1, 7, 0):
        arrive(xrecv.at[dz], d_sems.at[1 + dz])
        value = held[dz] + xrecv[dz].astype(jnp.float32)
        if dz:
            zsend[dz - 1] = value.astype(jnp.bfloat16)
            send(zsend.at[dz - 1], zrecv.at[dz - 1], d_sems.at[8 + dz], dz=dz)
        else:
            mine = value
    for dz in (1, 7, 2, 6, 3, 5, 4):
        arrive(zrecv.at[dz - 1], d_sems.at[8 + dz])
        mine = mine + zrecv[dz - 1].astype(jnp.float32)
    points = npt * NYL * NZ * NC
    out_ref[...] = mine[:, :m] * (1.0 / math.sqrt(points))
    for copy in sent:
        copy.wait_send()


def per_device(orbital_values, occupied, trial, point_weights, batch_sizes, significant):
    v, occ, tri = orbital_values.T, occupied.T, trial.T
    m, npt = v.shape
    nrow = occ.shape[0]
    half = 4 * nrow
    wide = (m + 127) // 128 * 128
    f32, bf16 = jnp.float32, jnp.bfloat16
    dma = pltpu.SemaphoreType.DMA
    out = pl.pallas_call(
        kernel,
        out_shape=jax.ShapeDtypeStruct((nrow, m), f32),
        in_specs=[pl.BlockSpec(memory_space=pl.ANY)] * 6,
        out_specs=pl.BlockSpec(memory_space=pltpu.VMEM),
        scratch_shapes=[
            pltpu.VMEM((m, npt), bf16),
            pltpu.VMEM((1, npt), f32),
            pltpu.VMEM((1, batch_sizes.shape[0]), jnp.int32),
            pltpu.VMEM(significant.shape, jnp.int32),
            pltpu.VMEM((2, nrow, m), bf16),
            pltpu.VMEM((4, 2, 4, nrow, wide), bf16),
            pltpu.VMEM((m, npt), bf16),
            pltpu.VMEM(significant.shape, jnp.int32),
            pltpu.VMEM((NC, wide, npt), bf16),
            pltpu.VMEM((NC, npt, wide), bf16),
            pltpu.VMEM((4, NX, 2 * half, 128), f32),
        ]
        + [
            pltpu.VMEM((4, NX - 1, 2 * half, 128), f32),
            pltpu.VMEM((4, NYH, CAP, 2 * half), f32),
            pltpu.VMEM((4, NYH - 1, CAP, 2 * half), f32),
            pltpu.VMEM((CAP, 2 * half), f32),
            pltpu.VMEM((CAP, 2 * half), f32),
            pltpu.VMEM((2, NX * NYH, CAP, 2 * half), bf16),
            pltpu.VMEM((NZ, nrow, wide), bf16),
            pltpu.VMEM((NZ, nrow, wide), bf16),
            pltpu.VMEM((NZ - 1, nrow, wide), bf16),
            pltpu.VMEM((NZ - 1, nrow, wide), bf16),
            dma((192,)),
            dma((64,)),
            dma((2,)),
            dma((4, NX - 1)),
            dma((4, NYH - 1)),
            dma((2, NX, NYH)),
            dma((1 + 8 + 8,)),
            dma((6,)),
        ]
        + [pltpu.SemaphoreType.REGULAR] * 5,
        compiler_params=pltpu.CompilerParams(
            collective_id=0, has_side_effects=True, vmem_limit_bytes=24 << 20
        ),
    )(*(
        pltpu.with_memory_space_constraint(a, pltpu.HBM)
        for a in (v, occ, tri, point_weights.reshape(1, -1), batch_sizes.reshape(1, -1), significant)
    ))
    return out.T


def solution(mesh):
    placed = (
        P("grid", "occ"),
        P("occ", "grid"),
        P("occ", "grid"),
        P("grid"),
        P("grid"),
        P("grid", "occ"),
    )
    return jax.shard_map(
        per_device, mesh=mesh, in_specs=placed, out_specs=P("occ", "grid"), check_vma=False
    )
```

```python
import functools
import math

import jax
import jax.numpy as jnp
from jax import lax
from jax.experimental import pallas as pl
from jax.experimental.pallas import tpu as pltpu
from jax.sharding import PartitionSpec as P

MESH = pl.DeviceIdType.MESH
NX, NYH, NYL, NZ, NC = 4, 4, 2, 8, 2
CAP = 32

SETS = (
    ((0, 0), (1, 0), (0, 1), (0, 7)),
    ((0, 2), (0, 6), (1, 1), (1, 7)),
    ((0, 4), (0, 3), (1, 2), (1, 6)),
    ((0, 5), (1, 4), (1, 3), (1, 5)),
)
WHERE = {slot: (s, i) for s, row in enumerate(SETS) for i, slot in enumerate(row)}


def kernel(
    v_hbm, occ_hbm, tri_hbm, w_hbm, sz_hbm, sig_hbm, out_ref,
    v_ref, w_ref, sz_ref, sig_ref, mine_ref, panels, vraw, sigp, stran, prod,
    xin, oin,
    turned, yrecv, dens_out, dens_in, kall,
    xsend, xrecv, zsend, zrecv,
    sems, p_sems, c_sems, x_sems, e_sems, o_sems, y_sems, k_sems, d_sems, l_sems,
    near, far, ready_x, ready_z, far_z, cross,
):
    g, o = lax.axis_index("grid"), lax.axis_index("occ")
    yl, z, c = g // (NZ * NC), (g // NC) % NZ, g % NC
    x, yh = o // NYH, o % NYH
    nrow = occ_hbm.shape[0]
    npt = v_ref.shape[1]

    def grid_at(dy, dz, dc):
        return (((yl + dy) % NYL) * NZ + (z + dz) % NZ) * NC + (c + dc) % NC

    def occ_at(dx, dyh):
        return ((x + dx) % NX) * NYH + (yh + dyh) % NYH

    sent = []

    def send(src, dst, recv_sem, dy=0, dz=0, dc=0, dx=0, dyh=0):
        copy = pltpu.make_async_remote_copy(
            src_ref=src, dst_ref=dst, send_sem=sems.at[len(sent)], recv_sem=recv_sem,
            device_id=at(dy, dz, dc, dx, dyh), device_id_type=MESH,
        )
        copy.start()
        sent.append(copy)

    def arrive(dst, recv_sem):
        pltpu.make_async_remote_copy(
            src_ref=dst, dst_ref=dst, send_sem=sems.at[0], recv_sem=recv_sem,
            device_id=at(dc=1), device_id_type=MESH,
        ).wait_recv()

    m, wide = v_hbm.shape[0], panels.shape[-1]
    loads = [
        pltpu.make_async_copy(src, dst, l_sems.at[n])
        for n, (src, dst) in enumerate((
            (occ_hbm, mine_ref.at[0]), (tri_hbm, mine_ref.at[1]), (sig_hbm, sig_ref),
            (v_hbm, v_ref), (w_hbm, w_ref), (sz_hbm, sz_ref),
        ))
    ]
    for load in loads:
        load.start()
    stran[:, :, m:] = jnp.zeros((NC, npt, wide - m), stran.dtype)

    def at(dy=0, dz=0, dc=0, dx=0, dyh=0):
        return {"grid": grid_at(dy, dz, dc), "occ": occ_at(dx, dyh)}

    def signal(sem, where):
        pl.semaphore_signal(sem, inc=1, device_id=where, device_id_type=MESH)

    beside = (at(dy=1, dyh=yl), at(dy=1, dyh=yl + NYH - 1))
    barrier = pltpu.get_barrier_semaphore()
    peers = (at(dc=1), at(dz=1), at(dz=7), at(dx=1), at(dx=3)) + beside
    for peer in peers:
        signal(barrier, peer)
    for load in loads:
        load.wait()
    panels[0, :, 0, :, :m] = mine_ref[...]
    panels[0, :, 0, :, m:] = jnp.zeros((2, nrow, wide - m), panels.dtype)
    pl.semaphore_wait(barrier, len(peers))
    for peer in beside:
        signal(near, peer)
    for peer in (at(dx=1), at(dx=3)):
        signal(ready_x, peer)
    for peer in (at(dz=1), at(dz=7)):
        signal(ready_z, peer)

    def place(slot, q):
        s, i = WHERE[slot]
        return panels.at[s, q // 2, i, :, pl.ds((q % 2) * (wide // 2), wide // 2)]

    def p_sem(slot, q):
        s, i = WHERE[slot]
        return p_sems.at[(s * 4 + i) * 4 + q]

    for q in range(4):
        send(place((0, 0), q), place((0, 7), q), p_sem((0, 7), q), dz=1)
        send(place((0, 0), q), place((0, 1), q), p_sem((0, 1), q), dz=7)
        send(place((0, 0), q), place((1, 0), q), p_sem((1, 0), q), dy=1)
    send(sig_hbm, sigp, c_sems.at[0], dc=1)
    send(v_hbm, vraw, c_sems.at[1], dc=1)
    pl.semaphore_wait(ready_z, 2)
    for step in (2, 6):
        signal(far_z, at(dz=step))

    def got(*slots):
        for slot in slots:
            for q in range(4):
                arrive(place(slot, q), p_sem(slot, q))

    def relay(slot, q, *moves):
        arrive(place(slot, q), p_sem(slot, q))
        for to, step in moves:
            send(place(slot, q), place(to, q), p_sem(to, q), **step)

    up, down, over = dict(dz=1), dict(dz=7), dict(dy=1)

    nblock, nbatch = sig_ref.shape[1], sig_ref.shape[0]
    width = v_ref.shape[0] // nblock

    def screen(values, significant):
        sig = significant.astype(jnp.float32).astype(jnp.bfloat16)
        eye = (
            lax.broadcasted_iota(jnp.int32, (nblock, nblock), 0)
            == lax.broadcasted_iota(jnp.int32, (nblock, nblock), 1)
        ).astype(jnp.bfloat16)
        flipped = lax.dot_general(
            eye, sig, (((1,), (1,)), ((), ())), preferred_element_type=jnp.float32
        ).astype(jnp.bfloat16)
        spread = (
            lax.broadcasted_iota(jnp.int32, (nbatch, npt), 1) // CAP
            == lax.broadcasted_iota(jnp.int32, (nbatch, npt), 0)
        ).astype(jnp.bfloat16)
        lanes = jnp.dot(flipped, spread, preferred_element_type=jnp.float32).astype(jnp.bfloat16)
        rows = (
            lax.broadcasted_iota(jnp.int32, (v_ref.shape[0], nblock), 0) // width
            == lax.broadcasted_iota(jnp.int32, (v_ref.shape[0], nblock), 1)
        ).astype(jnp.bfloat16)
        mask = jnp.dot(rows, lanes, preferred_element_type=jnp.float32)
        return values * mask.astype(jnp.bfloat16)

    stran[c, :, :m] = screen(v_ref[...], sig_ref[...]).T
    pl.semaphore_wait(near, 2)
    for k in (1, 3):
        signal(far, at(dyh=k))
    arrive(sigp, c_sems.at[0])
    arrive(vraw, c_sems.at[1])
    stran[1 - c, :, :m] = screen(vraw[...], sigp[...]).T
    pl.semaphore_wait(far_z, 2)
    for q in range(4):
        relay((0, 7), q, ((0, 6), up), ((1, 7), over), *([((0, 4), dict(dz=3))] if q < 2 else []))
        relay((0, 1), q, ((0, 2), down), ((1, 1), over), *([((0, 4), dict(dz=5))] if q > 1 else []))
    half = nrow * 4

    def multiply(s):
        panel = panels[s].reshape(2 * half, wide)
        for k in range(NC):
            res = lax.dot_general(
                stran[k], panel, (((1,), (1,)), ((), ())), preferred_element_type=jnp.float32
            )
            prod[s, 2 * k : 2 * k + 2] = res.reshape(2, NYH, CAP, 2 * half)

    def block(s, d, k):
        return prod.at[s, (x + d) % NX, (yh + k) % NYH]

    def x_first(s):
        for d in (2, 1, 3):
            send(prod.at[s, (x + d) % NX], xin.at[s, d - 1], x_sems.at[s, d - 1], dx=d)

    def x_last(s):
        for d in range(1, NX):
            arrive(xin.at[s, d - 1], x_sems.at[s, d - 1])
        turned[s] = prod[s, x] + xin[s, 0] + xin[s, 1] + xin[s, 2]
        for k in (2, 1, 3):
            send(turned.at[s, (yh + k) % NYH], yrecv.at[s, k - 1], y_sems.at[s, k - 1], dyh=k)

    def x_first_short(s):
        for d in (2, 1, 3, 0):
            send(block(s, d, 2), oin.at[d], o_sems.at[d], dx=d, dyh=2)
        for n, k in enumerate((1, 3, 0)):
            for d in (2, 1, 3):
                send(block(s, d, k), xin.at[s, d - 1, n], e_sems.at[d - 1, n], dx=d)

    def x_last_short(s):
        for n, k in enumerate((1, 3, 0)):
            for d in range(1, NX):
                arrive(xin.at[s, d - 1, n], e_sems.at[d - 1, n])
            turned[s, n] = prod[s, x, (yh + k) % NYH] + xin[s, 0, n] + xin[s, 1, n] + xin[s, 2, n]
            if k:
                send(turned.at[s, n], yrecv.at[s, k - 1], y_sems.at[s, k - 1], dyh=k)

    got((1, 0))
    pl.semaphore_wait(ready_x, 2)
    multiply(0)
    x_first(0)
    pl.semaphore_wait(far, 2)
    for d in (2, 1, 3):
        signal(cross, at(dx=d))
    for q in range(4):
        relay((0, 6), q, ((0, 5), up), ((1, 6), over))
        relay((0, 2), q, ((0, 3), down), ((1, 2), over))
        relay((1, 7), q, ((1, 5), dict(dz=2)))
        relay((1, 1), q, ((1, 3), dict(dz=6)))
    multiply(1)
    x_first(1)
    pl.semaphore_wait(cross, 3)
    for q in (2, 0, 1, 3):
        relay((0, 4), q, ((1, 4), over))
    got((1, 2), (1, 6), (0, 3))
    multiply(2)
    x_first(2)
    x_last(0)
    got((0, 5), (1, 4), (1, 5), (1, 3))
    multiply(3)
    x_first_short(3)
    x_last(1)
    x_last(2)
    x_last_short(3)

    lane = lax.broadcasted_iota(jnp.int32, (CAP, 2 * half), 1)
    units, rolled = [], []
    part = jnp.zeros((CAP, 1), jnp.float32)
    for s in range(4):
        unit = turned[s, yh] if s < 3 else turned[s, 2]
        for k in (1, 2, 3):
            if s < 3 or k != 2:
                arrive(yrecv.at[s, k - 1], y_sems.at[s, k - 1])
                unit = unit + yrecv[s, k - 1]
            else:
                for d in range(NX):
                    arrive(oin.at[d], o_sems.at[d])
                    unit = unit + oin[d]
        other = pltpu.roll(unit, half, 1)
        units.append(unit)
        rolled.append(other)
        part += jnp.sum(jnp.where(lane < half, unit * other, 0.0), axis=1, keepdims=True)

    batch = o % nbatch
    row_of = lax.broadcasted_iota(jnp.int32, (CAP, npt), 0)
    lane_of = lax.broadcasted_iota(jnp.int32, (CAP, npt), 1)
    weight = jnp.sum(
        jnp.where(lane_of == row_of + batch * CAP, w_ref[...], 0.0), axis=1, keepdims=True
    )
    count = jnp.sum(
        jnp.where(
            lax.broadcasted_iota(jnp.int32, (1, nbatch), 1) == batch,
            sz_ref[...].astype(jnp.float32), 0.0,
        ),
        axis=1, keepdims=True,
    )
    live = lax.broadcasted_iota(jnp.int32, (CAP, 1), 0).astype(jnp.float32) < count
    weight = jnp.where(live, weight, 0.0)
    dens_out[...] = jnp.where(lane < half, part, weight)
    send(dens_out, dens_in, d_sems.at[0], dc=1)
    arrive(dens_in, d_sems.at[0])
    total = 2 * nrow * NYL * NZ
    density = (part + dens_in[:, 0:1]) * (1.0 / math.sqrt(total))
    weight = jnp.where(o // nbatch == c, weight, dens_in[:, half : half + 1])
    for p in range(2):
        a, b = 2 * p, 2 * p + 1
        value = jnp.where(
            lane < half, density * units[a] + rolled[a], density * rolled[b] + units[b]
        )
        kall[p, o] = (weight * value).astype(jnp.bfloat16)

    def k_from(p, dx, dyh):
        return kall.at[p, occ_at(dx, dyh)]

    for p in (1, 0):
        for k in (2, 1, 3):
            send(k_from(p, 0, 0), k_from(p, 0, 0), k_sems.at[p, 0, NYH - k], dyh=k)
    for p in (1, 0):
        for k in (0, 1, 3, 2):
            if k:
                arrive(k_from(p, 0, k), k_sems.at[p, 0, k])
            for d in (2, 1, 3):
                send(k_from(p, 0, k), k_from(p, 0, k), k_sems.at[p, NX - d, k], dx=d)
    held = {}
    for p in (1, 0):
        for k in (0, 1, 3, 2):
            for d in (1, 3, 2):
                arrive(k_from(p, d, k), k_sems.at[p, d, k])
        kt = kall[p].reshape(2 * npt, 2 * half).T
        res = sum(
            jnp.dot(
                kt[:, k * npt : (k + 1) * npt], stran[k], preferred_element_type=jnp.float32
            )
            for k in range(NC)
        )
        slots = SETS[2 * p] + SETS[2 * p + 1]
        for dz in (4, 3, 5, 2, 6, 1, 7, 0):
            for dy in (1, 0):
                if (dy, dz) in slots:
                    i = slots.index((dy, dz))
                    block = res[i * nrow : (i + 1) * nrow]
                    if dy:
                        xsend[dz] = block.astype(jnp.bfloat16)
                        send(xsend.at[dz], xrecv.at[dz], d_sems.at[1 + dz], dy=1)
                    else:
                        held[dz] = block
    mine = None
    for dz in (4, 3, 5, 2, 6, 1, 7, 0):
        arrive(xrecv.at[dz], d_sems.at[1 + dz])
        value = held[dz] + xrecv[dz].astype(jnp.float32)
        if dz:
            zsend[dz - 1] = value.astype(jnp.bfloat16)
            send(zsend.at[dz - 1], zrecv.at[dz - 1], d_sems.at[8 + dz], dz=dz)
        else:
            mine = value
    for copy in sent:
        copy.wait_send()
    for dz in (1, 7, 2, 6, 3, 5, 4):
        arrive(zrecv.at[dz - 1], d_sems.at[8 + dz])
        mine = mine + zrecv[dz - 1].astype(jnp.float32)
    points = npt * NYL * NZ * NC
    out_ref[...] = mine[:, :m] * (1.0 / math.sqrt(points))


def per_device(orbital_values, occupied, trial, point_weights, batch_sizes, significant):
    v, occ, tri = orbital_values.T, occupied.T, trial.T
    m, npt = v.shape
    nrow = occ.shape[0]
    half = 4 * nrow
    wide = (m + 127) // 128 * 128
    f32, bf16 = jnp.float32, jnp.bfloat16
    dma = pltpu.SemaphoreType.DMA
    out = pl.pallas_call(
        kernel,
        out_shape=jax.ShapeDtypeStruct((nrow, m), f32),
        in_specs=[pl.BlockSpec(memory_space=pl.ANY)] * 6,
        out_specs=pl.BlockSpec(memory_space=pltpu.VMEM),
        scratch_shapes=[
            pltpu.VMEM((m, npt), bf16),
            pltpu.VMEM((1, npt), f32),
            pltpu.VMEM((1, batch_sizes.shape[0]), jnp.int32),
            pltpu.VMEM(significant.shape, jnp.int32),
            pltpu.VMEM((2, nrow, m), bf16),
            pltpu.VMEM((4, 2, 4, nrow, wide), bf16),
            pltpu.VMEM((m, npt), bf16),
            pltpu.VMEM(significant.shape, jnp.int32),
            pltpu.VMEM((NC, npt, wide), bf16),
            pltpu.VMEM((4, NX, NYH, CAP, 2 * half), f32),
        ]
        + [
            pltpu.VMEM((4, NX - 1, NYH, CAP, 2 * half), f32),
            pltpu.VMEM((NX, CAP, 2 * half), f32),
            pltpu.VMEM((4, NYH, CAP, 2 * half), f32),
            pltpu.VMEM((4, NYH - 1, CAP, 2 * half), f32),
            pltpu.VMEM((CAP, 2 * half), f32),
            pltpu.VMEM((CAP, 2 * half), f32),
            pltpu.VMEM((2, NX * NYH, CAP, 2 * half), bf16),
            pltpu.VMEM((NZ, nrow, wide), bf16),
            pltpu.VMEM((NZ, nrow, wide), bf16),
            pltpu.VMEM((NZ - 1, nrow, wide), bf16),
            pltpu.VMEM((NZ - 1, nrow, wide), bf16),
            dma((192,)),
            dma((64,)),
            dma((2,)),
            dma((3, NX - 1)),
            dma((NX - 1, 3)),
            dma((NX,)),
            dma((4, NYH - 1)),
            dma((2, NX, NYH)),
            dma((1 + 8 + 8,)),
            dma((6,)),
        ]
        + [pltpu.SemaphoreType.REGULAR] * 6,
        compiler_params=pltpu.CompilerParams(
            collective_id=0, has_side_effects=True, vmem_limit_bytes=24 << 20
        ),
    )(*(
        pltpu.with_memory_space_constraint(a, pltpu.HBM)
        for a in (v, occ, tri, point_weights.reshape(1, -1), batch_sizes.reshape(1, -1), significant)
    ))
    return out.T


def solution(mesh):
    placed = (
        P("grid", "occ"),
        P("occ", "grid"),
        P("occ", "grid"),
        P("grid"),
        P("grid"),
        P("grid", "occ"),
    )
    return jax.shard_map(
        per_device, mesh=mesh, in_specs=placed, out_specs=P("occ", "grid"), check_vma=False
    )
```

```python
import functools
import math

import jax
import jax.numpy as jnp
from jax import lax
from jax.experimental import pallas as pl
from jax.experimental.pallas import tpu as pltpu
from jax.sharding import PartitionSpec as P

MESH = pl.DeviceIdType.MESH
NX, NYH, NYL, NZ, NC = 4, 4, 2, 8, 2
CAP = 32

SETS = (
    ((0, 0), (1, 0), (0, 1), (0, 7)),
    ((0, 2), (0, 6), (1, 1), (1, 7)),
    ((0, 4), (0, 3), (1, 2), (1, 6)),
    ((0, 5), (1, 4), (1, 3), (1, 5)),
)
WHERE = {slot: (s, i) for s, row in enumerate(SETS) for i, slot in enumerate(row)}


def kernel(
    v_hbm, occ_hbm, tri_hbm, w_hbm, sz_hbm, sig_hbm, out_ref,
    v_ref, w_ref, sz_ref, sig_ref, mine_ref, panels, vraw, sigp, stran, prod,
    xin, oin,
    turned, yrecv, dens_out, dens_in, kall,
    xsend, xrecv, zsend, zrecv,
    sems, p_sems, c_sems, x_sems, e_sems, o_sems, y_sems, k_sems, d_sems, l_sems,
    near, far, ready_x, ready_z, far_z, cross,
):
    g, o = lax.axis_index("grid"), lax.axis_index("occ")
    yl, z, c = g // (NZ * NC), (g // NC) % NZ, g % NC
    x, yh = o // NYH, o % NYH
    nrow = occ_hbm.shape[0]
    npt = v_ref.shape[1]

    def grid_at(dy, dz, dc):
        return (((yl + dy) % NYL) * NZ + (z + dz) % NZ) * NC + (c + dc) % NC

    def occ_at(dx, dyh):
        return ((x + dx) % NX) * NYH + (yh + dyh) % NYH

    sent = []

    def send(src, dst, recv_sem, dy=0, dz=0, dc=0, dx=0, dyh=0):
        copy = pltpu.make_async_remote_copy(
            src_ref=src, dst_ref=dst, send_sem=sems.at[len(sent)], recv_sem=recv_sem,
            device_id=at(dy, dz, dc, dx, dyh), device_id_type=MESH,
        )
        copy.start()
        sent.append(copy)

    def arrive(dst, recv_sem):
        pltpu.make_async_remote_copy(
            src_ref=dst, dst_ref=dst, send_sem=sems.at[0], recv_sem=recv_sem,
            device_id=at(dc=1), device_id_type=MESH,
        ).wait_recv()

    m, wide = v_hbm.shape[0], panels.shape[-1]
    loads = [
        pltpu.make_async_copy(src, dst, l_sems.at[n])
        for n, (src, dst) in enumerate((
            (occ_hbm, mine_ref.at[0]), (tri_hbm, mine_ref.at[1]), (sig_hbm, sig_ref),
            (v_hbm, v_ref), (w_hbm, w_ref), (sz_hbm, sz_ref),
        ))
    ]
    for load in loads:
        load.start()

    def at(dy=0, dz=0, dc=0, dx=0, dyh=0):
        return {"grid": grid_at(dy, dz, dc), "occ": occ_at(dx, dyh)}

    def signal(sem, where):
        pl.semaphore_signal(sem, inc=1, device_id=where, device_id_type=MESH)

    beside = (at(dy=1, dyh=yl), at(dy=1, dyh=yl + NYH - 1))
    barrier = pltpu.get_barrier_semaphore()
    peers = (at(dc=1), at(dz=1), at(dz=7), at(dx=1), at(dx=3)) + beside
    for peer in peers:
        signal(barrier, peer)
    pl.semaphore_wait(barrier, len(peers))
    for peer in beside:
        signal(near, peer)
    for peer in (at(dx=1), at(dx=3)):
        signal(ready_x, peer)
    for peer in (at(dz=1), at(dz=7)):
        signal(ready_z, peer)

    def place(slot, q):
        s, i = WHERE[slot]
        return panels.at[s, q // 2, i, :, pl.ds((q % 2) * (wide // 2), wide // 2)]

    def p_sem(slot, q):
        s, i = WHERE[slot]
        return p_sems.at[(s * 4 + i) * 4 + q]

    def leave(own, q):
        send(own, place((0, 7), q), p_sem((0, 7), q), dz=1)
        send(own, place((0, 1), q), p_sem((0, 1), q), dz=7)
        send(own, place((1, 0), q), p_sem((1, 0), q), dy=1)

    leave(occ_hbm.at[:, pl.ds(0, wide // 2)], 0)
    leave(tri_hbm.at[:, pl.ds(0, wide // 2)], 2)
    for load in loads[:2]:
        load.wait()
    panels[0, :, 0, :, :m] = mine_ref[...]
    panels[0, :, 0, :, m:] = jnp.zeros((2, nrow, wide - m), panels.dtype)
    for q in (1, 3):
        leave(place((0, 0), q), q)
    send(sig_hbm, sigp, c_sems.at[0], dc=1)
    send(v_hbm, vraw, c_sems.at[1], dc=1)
    pl.semaphore_wait(ready_z, 2)
    for step in (2, 6):
        signal(far_z, at(dz=step))

    def got(*slots):
        for slot in slots:
            for q in range(4):
                arrive(place(slot, q), p_sem(slot, q))

    def relay(slot, q, *moves):
        arrive(place(slot, q), p_sem(slot, q))
        for to, step in moves:
            send(place(slot, q), place(to, q), p_sem(to, q), **step)

    up, down, over = dict(dz=1), dict(dz=7), dict(dy=1)

    nblock, nbatch = sig_ref.shape[1], sig_ref.shape[0]
    width = v_ref.shape[0] // nblock

    def screen(values, significant):
        sig = significant.astype(jnp.float32).astype(jnp.bfloat16)
        eye = (
            lax.broadcasted_iota(jnp.int32, (nblock, nblock), 0)
            == lax.broadcasted_iota(jnp.int32, (nblock, nblock), 1)
        ).astype(jnp.bfloat16)
        flipped = lax.dot_general(
            eye, sig, (((1,), (1,)), ((), ())), preferred_element_type=jnp.float32
        ).astype(jnp.bfloat16)
        spread = (
            lax.broadcasted_iota(jnp.int32, (nbatch, npt), 1) // CAP
            == lax.broadcasted_iota(jnp.int32, (nbatch, npt), 0)
        ).astype(jnp.bfloat16)
        lanes = jnp.dot(flipped, spread, preferred_element_type=jnp.float32).astype(jnp.bfloat16)
        rows = (
            lax.broadcasted_iota(jnp.int32, (v_ref.shape[0], nblock), 0) // width
            == lax.broadcasted_iota(jnp.int32, (v_ref.shape[0], nblock), 1)
        ).astype(jnp.bfloat16)
        mask = jnp.dot(rows, lanes, preferred_element_type=jnp.float32)
        return values * mask.astype(jnp.bfloat16)

    for load in loads[2:]:
        load.wait()
    stran[:, :, m:] = jnp.zeros((NC, npt, wide - m), stran.dtype)
    stran[c, :, :m] = screen(v_ref[...], sig_ref[...]).T
    pl.semaphore_wait(near, 2)
    for k in (1, 3):
        signal(far, at(dyh=k))
    arrive(sigp, c_sems.at[0])
    arrive(vraw, c_sems.at[1])
    stran[1 - c, :, :m] = screen(vraw[...], sigp[...]).T
    pl.semaphore_wait(far_z, 2)
    for q in (0, 2, 1, 3):
        relay((0, 7), q, ((0, 6), up), ((1, 7), over), *([((0, 4), dict(dz=3))] if q < 2 else []))
        relay((0, 1), q, ((0, 2), down), ((1, 1), over), *([((0, 4), dict(dz=5))] if q > 1 else []))
    half = nrow * 4

    def multiply(s):
        panel = panels[s].reshape(2 * half, wide)
        for k in range(NC):
            res = lax.dot_general(
                stran[k], panel, (((1,), (1,)), ((), ())), preferred_element_type=jnp.float32
            )
            prod[s, 2 * k : 2 * k + 2] = res.reshape(2, NYH, CAP, 2 * half)

    def block(s, d, k):
        return prod.at[s, (x + d) % NX, (yh + k) % NYH]

    def x_first(s):
        for d in (2, 1, 3):
            send(prod.at[s, (x + d) % NX], xin.at[s, d - 1], x_sems.at[s, d - 1], dx=d)

    def x_last(s):
        for d in range(1, NX):
            arrive(xin.at[s, d - 1], x_sems.at[s, d - 1])
        turned[s] = prod[s, x] + xin[s, 0] + xin[s, 1] + xin[s, 2]
        for k in (2, 1, 3):
            send(turned.at[s, (yh + k) % NYH], yrecv.at[s, k - 1], y_sems.at[s, k - 1], dyh=k)

    def x_first_short(s):
        for k in (1, 3, 2, 0):
            for d in (2, 1, 3) if k != 2 else (2, 1, 3, 0):
                if k == 2:
                    send(block(s, d, k), oin.at[d], o_sems.at[d], dx=d, dyh=2)
                else:
                    n = (1, 3, 0).index(k)
                    send(block(s, d, k), xin.at[s, d - 1, n], e_sems.at[d - 1, n], dx=d)

    def x_last_short(s):
        for n, k in enumerate((1, 3, 0)):
            for d in range(1, NX):
                arrive(xin.at[s, d - 1, n], e_sems.at[d - 1, n])
            turned[s, n] = prod[s, x, (yh + k) % NYH] + xin[s, 0, n] + xin[s, 1, n] + xin[s, 2, n]
            if k:
                send(turned.at[s, n], yrecv.at[s, k - 1], y_sems.at[s, k - 1], dyh=k)

    got((1, 0))
    pl.semaphore_wait(ready_x, 2)
    multiply(0)
    x_first(0)
    pl.semaphore_wait(far, 2)
    for d in (2, 1, 3):
        signal(cross, at(dx=d))
    for q in (0, 2, 1, 3):
        relay((0, 6), q, ((0, 5), up), ((1, 6), over))
        relay((0, 2), q, ((0, 3), down), ((1, 2), over))
        relay((1, 7), q, ((1, 5), dict(dz=2)))
        relay((1, 1), q, ((1, 3), dict(dz=6)))
    multiply(1)
    x_first(1)
    pl.semaphore_wait(cross, 3)
    for q in (0, 2, 1, 3):
        relay((0, 4), q, ((1, 4), over))
    got((1, 2), (1, 6), (0, 3))
    multiply(2)
    x_first(2)
    x_last(0)
    got((0, 5), (1, 4), (1, 5), (1, 3))
    multiply(3)
    x_first_short(3)
    x_last(1)
    x_last(2)
    x_last_short(3)

    lane = lax.broadcasted_iota(jnp.int32, (CAP, 2 * half), 1)
    units, rolled = [], []
    part = jnp.zeros((CAP, 1), jnp.float32)
    for s in range(4):
        unit = turned[s, yh] if s < 3 else turned[s, 2]
        for k in (1, 2, 3):
            if s < 3 or k != 2:
                arrive(yrecv.at[s, k - 1], y_sems.at[s, k - 1])
                unit = unit + yrecv[s, k - 1]
            else:
                for d in range(NX):
                    arrive(oin.at[d], o_sems.at[d])
                    unit = unit + oin[d]
        other = pltpu.roll(unit, half, 1)
        units.append(unit)
        rolled.append(other)
        part += jnp.sum(jnp.where(lane < half, unit * other, 0.0), axis=1, keepdims=True)

    batch = o % nbatch
    row_of = lax.broadcasted_iota(jnp.int32, (CAP, npt), 0)
    lane_of = lax.broadcasted_iota(jnp.int32, (CAP, npt), 1)
    weight = jnp.sum(
        jnp.where(lane_of == row_of + batch * CAP, w_ref[...], 0.0), axis=1, keepdims=True
    )
    count = jnp.sum(
        jnp.where(
            lax.broadcasted_iota(jnp.int32, (1, nbatch), 1) == batch,
            sz_ref[...].astype(jnp.float32), 0.0,
        ),
        axis=1, keepdims=True,
    )
    live = lax.broadcasted_iota(jnp.int32, (CAP, 1), 0).astype(jnp.float32) < count
    weight = jnp.where(live, weight, 0.0)
    dens_out[...] = jnp.where(lane < half, part, weight)
    send(dens_out, dens_in, d_sems.at[0], dc=1)
    arrive(dens_in, d_sems.at[0])
    total = 2 * nrow * NYL * NZ
    density = (part + dens_in[:, 0:1]) * (1.0 / math.sqrt(total))
    weight = jnp.where(o // nbatch == c, weight, dens_in[:, half : half + 1])
    for p in range(2):
        a, b = 2 * p, 2 * p + 1
        value = jnp.where(
            lane < half, density * units[a] + rolled[a], density * rolled[b] + units[b]
        )
        kall[p, o] = (weight * value).astype(jnp.bfloat16)

    def k_from(p, dx, dyh):
        return kall.at[p, occ_at(dx, dyh)]

    for p in (1, 0):
        for k in (2, 1, 3):
            send(k_from(p, 0, 0), k_from(p, 0, 0), k_sems.at[p, 0, NYH - k], dyh=k)
    for p in (1, 0):
        for k in (0, 1, 3, 2):
            if k:
                arrive(k_from(p, 0, k), k_sems.at[p, 0, k])
            for d in (2, 1, 3):
                send(k_from(p, 0, k), k_from(p, 0, k), k_sems.at[p, NX - d, k], dx=d)
    held = {}
    for p in (1, 0):
        for k in (0, 1, 3, 2):
            for d in (1, 3, 2):
                arrive(k_from(p, d, k), k_sems.at[p, d, k])
        kt = kall[p].reshape(2 * npt, 2 * half).T
        res = sum(
            jnp.dot(
                kt[:, k * npt : (k + 1) * npt], stran[k], preferred_element_type=jnp.float32
            )
            for k in range(NC)
        )
        slots = SETS[2 * p] + SETS[2 * p + 1]
        for dz in (4, 3, 5, 2, 6, 1, 7, 0):
            for dy in (1, 0):
                if (dy, dz) in slots:
                    i = slots.index((dy, dz))
                    block = res[i * nrow : (i + 1) * nrow]
                    if dy:
                        xsend[dz] = block.astype(jnp.bfloat16)
                        send(xsend.at[dz], xrecv.at[dz], d_sems.at[1 + dz], dy=1)
                    else:
                        held[dz] = block
    mine = None
    for dz in (4, 3, 5, 2, 6, 1, 7, 0):
        arrive(xrecv.at[dz], d_sems.at[1 + dz])
        value = held[dz] + xrecv[dz].astype(jnp.float32)
        if dz:
            zsend[dz - 1] = value.astype(jnp.bfloat16)
            send(zsend.at[dz - 1], zrecv.at[dz - 1], d_sems.at[8 + dz], dz=dz)
        else:
            mine = value
    for copy in sent:
        copy.wait_send()
    for dz in (1, 7, 2, 6, 3, 5, 4):
        arrive(zrecv.at[dz - 1], d_sems.at[8 + dz])
        mine = mine + zrecv[dz - 1].astype(jnp.float32)
    points = npt * NYL * NZ * NC
    out_ref[...] = mine[:, :m] * (1.0 / math.sqrt(points))


def per_device(orbital_values, occupied, trial, point_weights, batch_sizes, significant):
    v, occ, tri = orbital_values.T, occupied.T, trial.T
    m, npt = v.shape
    nrow = occ.shape[0]
    half = 4 * nrow
    wide = (m + 127) // 128 * 128
    f32, bf16 = jnp.float32, jnp.bfloat16
    dma = pltpu.SemaphoreType.DMA
    out = pl.pallas_call(
        kernel,
        out_shape=jax.ShapeDtypeStruct((nrow, m), f32),
        in_specs=[pl.BlockSpec(memory_space=pl.ANY)] * 6,
        out_specs=pl.BlockSpec(memory_space=pltpu.VMEM),
        scratch_shapes=[
            pltpu.VMEM((m, npt), bf16),
            pltpu.VMEM((1, npt), f32),
            pltpu.VMEM((1, batch_sizes.shape[0]), jnp.int32),
            pltpu.VMEM(significant.shape, jnp.int32),
            pltpu.VMEM((2, nrow, m), bf16),
            pltpu.VMEM((4, 2, 4, nrow, wide), bf16),
            pltpu.VMEM((m, npt), bf16),
            pltpu.VMEM(significant.shape, jnp.int32),
            pltpu.VMEM((NC, npt, wide), bf16),
            pltpu.VMEM((4, NX, NYH, CAP, 2 * half), f32),
        ]
        + [
            pltpu.VMEM((4, NX - 1, NYH, CAP, 2 * half), f32),
            pltpu.VMEM((NX, CAP, 2 * half), f32),
            pltpu.VMEM((4, NYH, CAP, 2 * half), f32),
            pltpu.VMEM((4, NYH - 1, CAP, 2 * half), f32),
            pltpu.VMEM((CAP, 2 * half), f32),
            pltpu.VMEM((CAP, 2 * half), f32),
            pltpu.VMEM((2, NX * NYH, CAP, 2 * half), bf16),
            pltpu.VMEM((NZ, nrow, wide), bf16),
            pltpu.VMEM((NZ, nrow, wide), bf16),
            pltpu.VMEM((NZ - 1, nrow, wide), bf16),
            pltpu.VMEM((NZ - 1, nrow, wide), bf16),
            dma((192,)),
            dma((64,)),
            dma((2,)),
            dma((3, NX - 1)),
            dma((NX - 1, 3)),
            dma((NX,)),
            dma((4, NYH - 1)),
            dma((2, NX, NYH)),
            dma((1 + 8 + 8,)),
            dma((6,)),
        ]
        + [pltpu.SemaphoreType.REGULAR] * 6,
        compiler_params=pltpu.CompilerParams(
            collective_id=0, has_side_effects=True, vmem_limit_bytes=24 << 20
        ),
    )(*(
        pltpu.with_memory_space_constraint(a, pltpu.HBM)
        for a in (v, occ, tri, point_weights.reshape(1, -1), batch_sizes.reshape(1, -1), significant)
    ))
    return out.T


def solution(mesh):
    placed = (
        P("grid", "occ"),
        P("occ", "grid"),
        P("occ", "grid"),
        P("grid"),
        P("grid"),
        P("grid", "occ"),
    )
    return jax.shard_map(
        per_device, mesh=mesh, in_specs=placed, out_specs=P("occ", "grid"), check_vma=False
    )
```

```python
import functools
import math

import jax
import jax.numpy as jnp
from jax import lax
from jax.experimental import pallas as pl
from jax.experimental.pallas import tpu as pltpu
from jax.sharding import PartitionSpec as P

MESH = pl.DeviceIdType.MESH
NX, NYH, NYL, NZ, NC = 4, 4, 2, 8, 2
CAP = 32

SETS = (
    ((0, 0), (1, 0), (0, 1), (0, 7)),
    ((0, 2), (0, 6), (1, 1), (1, 7)),
    ((0, 4), (0, 3), (1, 2), (1, 6)),
    ((0, 5), (1, 4), (1, 3), (1, 5)),
)
RELAYED = ((0, 7), (0, 1), (0, 6), (0, 2), (1, 7), (1, 1), (0, 4))
WHERE = {slot: (s, i) for s, row in enumerate(SETS) for i, slot in enumerate(row)}


def kernel(
    v_hbm, occ_hbm, tri_hbm, w_hbm, sz_hbm, sig_hbm, out_ref,
    v_ref, w_ref, sz_ref, sig_ref, mine_ref, panels, vraw, sigp, stran, prod,
    xin, oin,
    turned, yrecv, dens_out, dens_in, kall,
    xsend, xrecv, zsend, zrecv,
    sems, p_sems, g_sems, c_sems, x_sems, e_sems, o_sems, y_sems, k_sems, d_sems, l_sems,
    near, far, ready_x, ready_z, far_z, cross,
):
    g, o = lax.axis_index("grid"), lax.axis_index("occ")
    yl, z, c = g // (NZ * NC), (g // NC) % NZ, g % NC
    x, yh = o // NYH, o % NYH
    nrow = occ_hbm.shape[0]
    npt = v_ref.shape[1]

    def grid_at(dy, dz, dc):
        return (((yl + dy) % NYL) * NZ + (z + dz) % NZ) * NC + (c + dc) % NC

    def occ_at(dx, dyh):
        return ((x + dx) % NX) * NYH + (yh + dyh) % NYH

    amount = {}

    def send(src, dst, recv_sem, group, **where):
        pltpu.make_async_remote_copy(
            src_ref=src, dst_ref=dst, send_sem=sems.at[group], recv_sem=recv_sem,
            device_id=at(**where), device_id_type=MESH,
        ).start()
        amount[group] = amount.get(group, 0) + math.prod(src.shape) * src.dtype.itemsize

    def all_sent(group, ref):
        assert amount[group] == math.prod(ref.shape) * ref.dtype.itemsize
        pltpu.make_async_remote_copy(
            src_ref=ref, dst_ref=ref, send_sem=sems.at[group], recv_sem=sems.at[group],
            device_id=at(dc=1), device_id_type=MESH,
        ).wait_send()

    def arrive(dst, recv_sem):
        pltpu.make_async_remote_copy(
            src_ref=dst, dst_ref=dst, send_sem=sems.at[0], recv_sem=recv_sem,
            device_id=at(dc=1), device_id_type=MESH,
        ).wait_recv()

    m, wide = v_hbm.shape[0], panels.shape[-1]
    loads = [
        pltpu.make_async_copy(src, dst, l_sems.at[n])
        for n, (src, dst) in enumerate((
            (occ_hbm, mine_ref.at[0]), (tri_hbm, mine_ref.at[1]), (sig_hbm, sig_ref),
            (v_hbm, v_ref), (w_hbm, w_ref), (sz_hbm, sz_ref),
        ))
    ]
    for load in loads:
        load.start()

    def at(dy=0, dz=0, dc=0, dx=0, dyh=0):
        return {"grid": grid_at(dy, dz, dc), "occ": occ_at(dx, dyh)}

    def signal(sem, where):
        pl.semaphore_signal(sem, inc=1, device_id=where, device_id_type=MESH)

    beside = (at(dy=1, dyh=yl), at(dy=1, dyh=yl + NYH - 1))
    barrier = pltpu.get_barrier_semaphore()
    peers = (at(dc=1), at(dz=1), at(dz=7), at(dx=1), at(dx=3)) + beside
    for peer in peers:
        signal(barrier, peer)
    pl.semaphore_wait(barrier, len(peers))
    for peer in beside:
        signal(near, peer)
    for peer in (at(dx=1), at(dx=3)):
        signal(ready_x, peer)
    for peer in (at(dz=1), at(dz=7)):
        signal(ready_z, peer)

    def place(slot, q):
        s, i = WHERE[slot]
        return panels.at[s, q // 2, i, :, pl.ds((q % 2) * (wide // 2), wide // 2)]

    def p_sem(slot, q):
        s, i = WHERE[slot]
        return p_sems.at[RELAYED.index(slot) * 4 + q] if slot in RELAYED else g_sems.at[s * 4 + i]

    def leave(own, q):
        send(own, place((0, 7), q), p_sem((0, 7), q), 1, dz=1)
        send(own, place((0, 1), q), p_sem((0, 1), q), 1, dz=7)
        send(own, place((1, 0), q), p_sem((1, 0), q), 1, dy=1)

    leave(occ_hbm.at[:, pl.ds(0, wide // 2)], 0)
    leave(tri_hbm.at[:, pl.ds(0, wide // 2)], 2)
    for load in loads[:2]:
        load.wait()
    panels[0, :, 0, :, :m] = mine_ref[...]
    panels[0, :, 0, :, m:] = jnp.zeros((2, nrow, wide - m), panels.dtype)
    for q in (1, 3):
        leave(place((0, 0), q), q)
    send(sig_hbm, sigp, c_sems.at[0], 2, dc=1)
    send(v_hbm, vraw, c_sems.at[1], 3, dc=1)
    pl.semaphore_wait(ready_z, 2)
    for step in (2, 6):
        signal(far_z, at(dz=step))

    def got(*slots):
        for slot in slots:
            s, i = WHERE[slot]
            arrive(panels.at[s, :, i], p_sem(slot, 0))

    def relay(slot, q, *moves):
        arrive(place(slot, q), p_sem(slot, q))
        for to, step in moves:
            send(place(slot, q), place(to, q), p_sem(to, q), 0, **step)

    up, down, over = dict(dz=1), dict(dz=7), dict(dy=1)

    nblock, nbatch = sig_ref.shape[1], sig_ref.shape[0]
    width = v_ref.shape[0] // nblock

    def screen(values, significant):
        sig = significant.astype(jnp.float32).astype(jnp.bfloat16)
        eye = (
            lax.broadcasted_iota(jnp.int32, (nblock, nblock), 0)
            == lax.broadcasted_iota(jnp.int32, (nblock, nblock), 1)
        ).astype(jnp.bfloat16)
        flipped = lax.dot_general(
            eye, sig, (((1,), (1,)), ((), ())), preferred_element_type=jnp.float32
        ).astype(jnp.bfloat16)
        spread = (
            lax.broadcasted_iota(jnp.int32, (nbatch, npt), 1) // CAP
            == lax.broadcasted_iota(jnp.int32, (nbatch, npt), 0)
        ).astype(jnp.bfloat16)
        lanes = jnp.dot(flipped, spread, preferred_element_type=jnp.float32).astype(jnp.bfloat16)
        rows = (
            lax.broadcasted_iota(jnp.int32, (v_ref.shape[0], nblock), 0) // width
            == lax.broadcasted_iota(jnp.int32, (v_ref.shape[0], nblock), 1)
        ).astype(jnp.bfloat16)
        mask = jnp.dot(rows, lanes, preferred_element_type=jnp.float32)
        return values * mask.astype(jnp.bfloat16)

    for load in loads[2:]:
        load.wait()
    stran[:, :, m:] = jnp.zeros((NC, npt, wide - m), stran.dtype)
    stran[c, :, :m] = screen(v_ref[...], sig_ref[...]).T
    pl.semaphore_wait(near, 2)
    for k in (1, 3):
        signal(far, at(dyh=k))
    arrive(sigp, c_sems.at[0])
    arrive(vraw, c_sems.at[1])
    stran[1 - c, :, :m] = screen(vraw[...], sigp[...]).T
    pl.semaphore_wait(far_z, 2)
    for q in (0, 2, 1, 3):
        relay((0, 7), q, ((0, 6), up), ((1, 7), over), *([((0, 4), dict(dz=3))] if q < 2 else []))
        relay((0, 1), q, ((0, 2), down), ((1, 1), over), *([((0, 4), dict(dz=5))] if q > 1 else []))
    half = nrow * 4

    def multiply(s):
        panel = panels[s].reshape(2 * half, wide)
        for k in range(NC):
            res = lax.dot_general(
                stran[k], panel, (((1,), (1,)), ((), ())), preferred_element_type=jnp.float32
            )
            prod[s, 2 * k : 2 * k + 2] = res.reshape(2, NYH, CAP, 2 * half)

    def block(s, d, k):
        return prod.at[s, (x + d) % NX, (yh + k) % NYH]

    def x_first(s):
        for d in (2, 1, 3):
            send(prod.at[s, (x + d) % NX], xin.at[s, d - 1], x_sems.at[s], 4, dx=d)

    def x_last(s):
        arrive(xin.at[s], x_sems.at[s])
        turned[s] = prod[s, x] + xin[s, 0] + xin[s, 1] + xin[s, 2]
        for k in (2, 1, 3):
            send(turned.at[s, (yh + k) % NYH], yrecv.at[s, k - 1], y_sems.at[s], 5, dyh=k)

    def x_first_short(s):
        for k in (1, 3, 2, 0):
            for d in (2, 1, 3) if k != 2 else (2, 1, 3, 0):
                if k == 2:
                    send(block(s, d, k), oin.at[d], o_sems.at[0], 6, dx=d, dyh=2)
                else:
                    n = (1, 3, 0).index(k)
                    send(block(s, d, k), xin.at[s, d - 1, n], e_sems.at[n], 7, dx=d)

    def x_last_short(s):
        for n, k in enumerate((1, 3, 0)):
            arrive(xin.at[s, :, n], e_sems.at[n])
            turned[s, n] = prod[s, x, (yh + k) % NYH] + xin[s, 0, n] + xin[s, 1, n] + xin[s, 2, n]
            if k:
                send(turned.at[s, n], yrecv.at[s, n], y_sems.at[s], 8, dyh=k)

    got((1, 0))
    pl.semaphore_wait(ready_x, 2)
    multiply(0)
    x_first(0)
    pl.semaphore_wait(far, 2)
    for d in (2, 1, 3):
        signal(cross, at(dx=d))
    for q in (0, 2, 1, 3):
        relay((0, 6), q, ((0, 5), up), ((1, 6), over))
        relay((0, 2), q, ((0, 3), down), ((1, 2), over))
        relay((1, 7), q, ((1, 5), dict(dz=2)))
        relay((1, 1), q, ((1, 3), dict(dz=6)))
    multiply(1)
    x_first(1)
    pl.semaphore_wait(cross, 3)
    for q in (0, 2, 1, 3):
        relay((0, 4), q, ((1, 4), over))
    got((1, 2), (1, 6), (0, 3))
    multiply(2)
    x_first(2)
    x_last(0)
    got((0, 5), (1, 4), (1, 5), (1, 3))
    multiply(3)
    x_first_short(3)
    x_last(1)
    x_last(2)
    x_last_short(3)

    lane = lax.broadcasted_iota(jnp.int32, (CAP, 2 * half), 1)
    units, rolled = [], []
    part = jnp.zeros((CAP, 1), jnp.float32)
    for s in range(4):
        unit = turned[s, yh] if s < 3 else turned[s, 2]
        if s < 3:
            arrive(yrecv.at[s], y_sems.at[s])
            unit = unit + yrecv[s, 0] + yrecv[s, 1] + yrecv[s, 2]
        else:
            arrive(oin, o_sems.at[0])
            unit = unit + oin[0] + oin[1] + oin[2] + oin[3]
            arrive(yrecv.at[s, pl.ds(0, 2)], y_sems.at[s])
            unit = unit + yrecv[s, 0] + yrecv[s, 1]
        other = pltpu.roll(unit, half, 1)
        units.append(unit)
        rolled.append(other)
        part += jnp.sum(jnp.where(lane < half, unit * other, 0.0), axis=1, keepdims=True)

    batch = o % nbatch
    row_of = lax.broadcasted_iota(jnp.int32, (CAP, npt), 0)
    lane_of = lax.broadcasted_iota(jnp.int32, (CAP, npt), 1)
    weight = jnp.sum(
        jnp.where(lane_of == row_of + batch * CAP, w_ref[...], 0.0), axis=1, keepdims=True
    )
    count = jnp.sum(
        jnp.where(
            lax.broadcasted_iota(jnp.int32, (1, nbatch), 1) == batch,
            sz_ref[...].astype(jnp.float32), 0.0,
        ),
        axis=1, keepdims=True,
    )
    live = lax.broadcasted_iota(jnp.int32, (CAP, 1), 0).astype(jnp.float32) < count
    weight = jnp.where(live, weight, 0.0)
    dens_out[...] = jnp.where(lane < half, part, weight)
    send(dens_out, dens_in, d_sems.at[0], 9, dc=1)
    arrive(dens_in, d_sems.at[0])
    total = 2 * nrow * NYL * NZ
    density = (part + dens_in[:, 0:1]) * (1.0 / math.sqrt(total))
    weight = jnp.where(o // nbatch == c, weight, dens_in[:, half : half + 1])
    for p in range(2):
        a, b = 2 * p, 2 * p + 1
        value = jnp.where(
            lane < half, density * units[a] + rolled[a], density * rolled[b] + units[b]
        )
        kall[p, o] = (weight * value).astype(jnp.bfloat16)

    def k_from(p, dx, dyh):
        return kall.at[p, occ_at(dx, dyh)]

    for p in (1, 0):
        for k in (2, 1, 3):
            send(k_from(p, 0, 0), k_from(p, 0, 0), k_sems.at[p, NYH - k], 10, dyh=k)
    for p in (1, 0):
        for k in (0, 1, 3, 2):
            if k:
                arrive(k_from(p, 0, k), k_sems.at[p, k])
            for d in (2, 1, 3):
                send(k_from(p, 0, k), k_from(p, 0, k), k_sems.at[p, 0], 10, dx=d)
    held = {}
    for p in (1, 0):
        arrive(kall.at[p, pl.ds(0, (NX - 1) * NYH)], k_sems.at[p, 0])
        kt = kall[p].reshape(2 * npt, 2 * half).T
        res = sum(
            jnp.dot(
                kt[:, k * npt : (k + 1) * npt], stran[k], preferred_element_type=jnp.float32
            )
            for k in range(NC)
        )
        slots = SETS[2 * p] + SETS[2 * p + 1]
        for dz in (4, 3, 5, 2, 6, 1, 7, 0):
            for dy in (1, 0):
                if (dy, dz) in slots:
                    i = slots.index((dy, dz))
                    block = res[i * nrow : (i + 1) * nrow]
                    if dy:
                        xsend[dz] = block.astype(jnp.bfloat16)
                        send(xsend.at[dz], xrecv.at[dz], d_sems.at[1 + dz], 11, dy=1)
                    else:
                        held[dz] = block
    mine = None
    for dz in (4, 3, 5, 2, 6, 1, 7, 0):
        arrive(xrecv.at[dz], d_sems.at[1 + dz])
        value = held[dz] + xrecv[dz].astype(jnp.float32)
        if dz:
            zsend[dz - 1] = value.astype(jnp.bfloat16)
            send(zsend.at[dz - 1], zrecv.at[dz - 1], d_sems.at[8 + dz], 12, dz=dz)
        else:
            mine = value
    for group, ref in enumerate((
        panels.at[pl.ds(0, 3)], panels.at[0, :, pl.ds(0, 3)], sigp, vraw, xin.at[pl.ds(0, 3)],
        yrecv.at[pl.ds(0, 3)], oin, xin.at[3, :, pl.ds(0, 3)], yrecv.at[3, pl.ds(0, 2)], dens_in,
        kall.at[:, pl.ds(0, 15)], xsend, zsend,
    )):
        all_sent(group, ref)
    for dz in (1, 7, 2, 6, 3, 5, 4):
        arrive(zrecv.at[dz - 1], d_sems.at[8 + dz])
        mine = mine + zrecv[dz - 1].astype(jnp.float32)
    points = npt * NYL * NZ * NC
    out_ref[...] = mine[:, :m] * (1.0 / math.sqrt(points))


def per_device(orbital_values, occupied, trial, point_weights, batch_sizes, significant):
    v, occ, tri = orbital_values.T, occupied.T, trial.T
    m, npt = v.shape
    nrow = occ.shape[0]
    half = 4 * nrow
    wide = (m + 127) // 128 * 128
    f32, bf16 = jnp.float32, jnp.bfloat16
    dma = pltpu.SemaphoreType.DMA
    out = pl.pallas_call(
        kernel,
        out_shape=jax.ShapeDtypeStruct((nrow, m), f32),
        in_specs=[pl.BlockSpec(memory_space=pl.ANY)] * 6,
        out_specs=pl.BlockSpec(memory_space=pltpu.VMEM),
        scratch_shapes=[
            pltpu.VMEM((m, npt), bf16),
            pltpu.VMEM((1, npt), f32),
            pltpu.VMEM((1, batch_sizes.shape[0]), jnp.int32),
            pltpu.VMEM(significant.shape, jnp.int32),
            pltpu.VMEM((2, nrow, m), bf16),
            pltpu.VMEM((4, 2, 4, nrow, wide), bf16),
            pltpu.VMEM((m, npt), bf16),
            pltpu.VMEM(significant.shape, jnp.int32),
            pltpu.VMEM((NC, npt, wide), bf16),
            pltpu.VMEM((4, NX, NYH, CAP, 2 * half), f32),
        ]
        + [
            pltpu.VMEM((4, NX - 1, NYH, CAP, 2 * half), f32),
            pltpu.VMEM((NX, CAP, 2 * half), f32),
            pltpu.VMEM((4, NYH, CAP, 2 * half), f32),
            pltpu.VMEM((4, NYH - 1, CAP, 2 * half), f32),
            pltpu.VMEM((CAP, 2 * half), f32),
            pltpu.VMEM((CAP, 2 * half), f32),
            pltpu.VMEM((2, NX * NYH, CAP, 2 * half), bf16),
            pltpu.VMEM((NZ, nrow, wide), bf16),
            pltpu.VMEM((NZ, nrow, wide), bf16),
            pltpu.VMEM((NZ - 1, nrow, wide), bf16),
            pltpu.VMEM((NZ - 1, nrow, wide), bf16),
            dma((13,)),
            dma((28,)),
            dma((16,)),
            dma((2,)),
            dma((3,)),
            dma((3,)),
            dma((1,)),
            dma((4,)),
            dma((2, NYH)),
            dma((1 + 8 + 8,)),
            dma((6,)),
        ]
        + [pltpu.SemaphoreType.REGULAR] * 6,
        compiler_params=pltpu.CompilerParams(
            collective_id=0, has_side_effects=True, vmem_limit_bytes=24 << 20
        ),
    )(*(
        pltpu.with_memory_space_constraint(a, pltpu.HBM)
        for a in (v, occ, tri, point_weights.reshape(1, -1), batch_sizes.reshape(1, -1), significant)
    ))
    return out.T


def solution(mesh):
    placed = (
        P("grid", "occ"),
        P("occ", "grid"),
        P("occ", "grid"),
        P("grid"),
        P("grid"),
        P("grid", "occ"),
    )
    return jax.shard_map(
        per_device, mesh=mesh, in_specs=placed, out_specs=P("occ", "grid"), check_vma=False
    )
```

```python
import functools
import math

import jax
import jax.numpy as jnp
from jax import lax
from jax.experimental import pallas as pl
from jax.experimental.pallas import tpu as pltpu
from jax.sharding import PartitionSpec as P

MESH = pl.DeviceIdType.MESH
NX, NYH, NYL, NZ, NC = 4, 4, 2, 8, 2
CAP = 32

SETS = (
    ((0, 0), (1, 0), (0, 1), (0, 7)),
    ((0, 2), (0, 6), (1, 1), (1, 7)),
    ((0, 4), (0, 3), (1, 2), (1, 6)),
    ((0, 5), (1, 4), (1, 3), (1, 5)),
)
RELAYED = ((0, 7), (0, 1), (0, 6), (0, 2), (1, 7), (1, 1), (0, 4))
GOT = ((1, 0), (1, 2), (1, 6), (0, 3), (0, 5), (1, 4), (1, 3), (1, 5))
WHERE = {slot: (s, i) for s, row in enumerate(SETS) for i, slot in enumerate(row)}


def kernel(
    v_hbm, occ_hbm, tri_hbm, w_hbm, sz_hbm, sig_hbm, out_ref,
    v_ref, w_ref, sz_ref, sig_ref, mine_ref, panels, vraw, sigp, stran, prod,
    xin, oin,
    turned, yrecv, dens_out, dens_in, kall,
    xsend, xrecv, zsend, zrecv,
    sems, p_sems, g_sems, c_sems, x_sems, e_sems, o_sems, y_sems, k_sems, d_sems, l_sems,
    near, far, ready_x, ready_z, far_z, cross,
):
    g, o = lax.axis_index("grid"), lax.axis_index("occ")
    yl, z, c = g // (NZ * NC), (g // NC) % NZ, g % NC
    x, yh = o // NYH, o % NYH
    nrow = occ_hbm.shape[0]
    npt = v_ref.shape[1]

    def grid_at(dy, dz, dc):
        return (((yl + dy) % NYL) * NZ + (z + dz) % NZ) * NC + (c + dc) % NC

    def occ_at(dx, dyh):
        return ((x + dx) % NX) * NYH + (yh + dyh) % NYH

    amount = {}

    def send(src, dst, recv_sem, group, **where):
        pltpu.make_async_remote_copy(
            src_ref=src, dst_ref=dst, send_sem=sems.at[group], recv_sem=recv_sem,
            device_id=at(**where), device_id_type=MESH,
        ).start()
        amount[group] = amount.get(group, 0) + math.prod(src.shape) * src.dtype.itemsize

    def all_sent(group, ref):
        assert amount[group] == math.prod(ref.shape) * ref.dtype.itemsize
        pltpu.make_async_remote_copy(
            src_ref=ref, dst_ref=ref, send_sem=sems.at[group], recv_sem=sems.at[group],
            device_id=at(dc=1), device_id_type=MESH,
        ).wait_send()

    def arrive(dst, recv_sem):
        pltpu.make_async_remote_copy(
            src_ref=dst, dst_ref=dst, send_sem=sems.at[0], recv_sem=recv_sem,
            device_id=at(dc=1), device_id_type=MESH,
        ).wait_recv()

    m, wide = v_hbm.shape[0], panels.shape[-1]
    loads = [
        pltpu.make_async_copy(src, dst, l_sems.at[n])
        for n, (src, dst) in enumerate((
            (occ_hbm, mine_ref.at[0]), (tri_hbm, mine_ref.at[1]), (sig_hbm, sig_ref),
            (v_hbm, v_ref), (w_hbm, w_ref), (sz_hbm, sz_ref),
        ))
    ]
    for load in loads:
        load.start()

    def at(dy=0, dz=0, dc=0, dx=0, dyh=0):
        return {"grid": grid_at(dy, dz, dc), "occ": occ_at(dx, dyh)}

    def signal(sem, where):
        pl.semaphore_signal(sem, inc=1, device_id=where, device_id_type=MESH)

    beside = (at(dy=1, dyh=yl), at(dy=1, dyh=yl + NYH - 1))
    barrier = pltpu.get_barrier_semaphore()
    peers = (at(dc=1), at(dz=1), at(dz=7), at(dx=1), at(dx=3)) + beside
    for peer in peers:
        signal(barrier, peer)
    pl.semaphore_wait(barrier, len(peers))
    for peer in beside:
        signal(near, peer)
    for peer in (at(dx=1), at(dx=3)):
        signal(ready_x, peer)
    for peer in (at(dz=1), at(dz=7)):
        signal(ready_z, peer)

    def place(slot, q):
        s, i = WHERE[slot]
        return panels.at[s, q // 2, i, :, pl.ds((q % 2) * (wide // 2), wide // 2)]

    def p_sem(slot, q):
        s, i = WHERE[slot]
        return p_sems.at[RELAYED.index(slot) * 4 + q] if slot in RELAYED else g_sems.at[GOT.index(slot)]

    def leave(own, q):
        send(own, place((0, 7), q), p_sem((0, 7), q), 1, dz=1)
        send(own, place((0, 1), q), p_sem((0, 1), q), 1, dz=7)
        send(own, place((1, 0), q), p_sem((1, 0), q), 1, dy=1)

    leave(occ_hbm.at[:, pl.ds(0, wide // 2)], 0)
    leave(tri_hbm.at[:, pl.ds(0, wide // 2)], 2)
    for load in loads[:2]:
        load.wait()
    panels[0, :, 0, :, :m] = mine_ref[...]
    panels[0, :, 0, :, m:] = jnp.zeros((2, nrow, wide - m), panels.dtype)
    for q in (1, 3):
        leave(place((0, 0), q), q)
    send(sig_hbm, sigp, c_sems.at[0], 2, dc=1)
    send(v_hbm, vraw, c_sems.at[1], 3, dc=1)
    pl.semaphore_wait(ready_z, 2)
    for step in (2, 6):
        signal(far_z, at(dz=step))

    def got(*slots):
        for slot in slots:
            s, i = WHERE[slot]
            arrive(panels.at[s, :, i], p_sem(slot, 0))

    def relay(slot, q, *moves):
        arrive(place(slot, q), p_sem(slot, q))
        for to, step in moves:
            send(place(slot, q), place(to, q), p_sem(to, q), 0, **step)

    up, down, over = dict(dz=1), dict(dz=7), dict(dy=1)

    nblock, nbatch = sig_ref.shape[1], sig_ref.shape[0]
    width = v_ref.shape[0] // nblock

    def screen(values, significant):
        sig = significant.astype(jnp.float32).astype(jnp.bfloat16)
        eye = (
            lax.broadcasted_iota(jnp.int32, (nblock, nblock), 0)
            == lax.broadcasted_iota(jnp.int32, (nblock, nblock), 1)
        ).astype(jnp.bfloat16)
        flipped = lax.dot_general(
            eye, sig, (((1,), (1,)), ((), ())), preferred_element_type=jnp.float32
        ).astype(jnp.bfloat16)
        spread = (
            lax.broadcasted_iota(jnp.int32, (nbatch, npt), 1) // CAP
            == lax.broadcasted_iota(jnp.int32, (nbatch, npt), 0)
        ).astype(jnp.bfloat16)
        lanes = jnp.dot(flipped, spread, preferred_element_type=jnp.float32).astype(jnp.bfloat16)
        rows = (
            lax.broadcasted_iota(jnp.int32, (v_ref.shape[0], nblock), 0) // width
            == lax.broadcasted_iota(jnp.int32, (v_ref.shape[0], nblock), 1)
        ).astype(jnp.bfloat16)
        mask = jnp.dot(rows, lanes, preferred_element_type=jnp.float32)
        return values * mask.astype(jnp.bfloat16)

    for load in loads[2:]:
        load.wait()
    stran[:, :, m:] = jnp.zeros((NC, npt, wide - m), stran.dtype)
    stran[c, :, :m] = screen(v_ref[...], sig_ref[...]).T
    pl.semaphore_wait(near, 2)
    for k in (1, 3):
        signal(far, at(dyh=k))
    arrive(sigp, c_sems.at[0])
    arrive(vraw, c_sems.at[1])
    stran[1 - c, :, :m] = screen(vraw[...], sigp[...]).T
    pl.semaphore_wait(far_z, 2)
    for q in (0, 2, 1, 3):
        relay((0, 7), q, ((0, 6), up), ((1, 7), over), *([((0, 4), dict(dz=3))] if q < 2 else []))
        relay((0, 1), q, ((0, 2), down), ((1, 1), over), *([((0, 4), dict(dz=5))] if q > 1 else []))
    half = nrow * 4

    def multiply(s):
        panel = panels[s].reshape(2 * half, wide)
        for k in range(NC):
            res = lax.dot_general(
                stran[k], panel, (((1,), (1,)), ((), ())), preferred_element_type=jnp.float32
            )
            prod[s, 2 * k : 2 * k + 2] = res.reshape(2, NYH, CAP, 2 * half)

    def block(s, d, k):
        return prod.at[s, (x + d) % NX, (yh + k) % NYH]

    def x_first(s):
        for d in (2, 1, 3):
            send(prod.at[s, (x + d) % NX], xin.at[s, d - 1], x_sems.at[s], 4, dx=d)

    def x_last(s):
        arrive(xin.at[s], x_sems.at[s])
        turned[s] = prod[s, x] + xin[s, 0] + xin[s, 1] + xin[s, 2]
        for k in (2, 1, 3):
            send(turned.at[s, (yh + k) % NYH], yrecv.at[s, k - 1], y_sems.at[s], 5, dyh=k)

    def x_first_short(s):
        for k in (1, 3, 2, 0):
            for d in (2, 1, 3) if k != 2 else (2, 1, 3, 0):
                if k == 2:
                    send(block(s, d, k), oin.at[d], o_sems.at[0], 6, dx=d, dyh=2)
                else:
                    n = (1, 3, 0).index(k)
                    send(block(s, d, k), xin.at[s, d - 1, n], e_sems.at[n], 7, dx=d)

    def x_last_short(s):
        for n, k in enumerate((1, 3, 0)):
            arrive(xin.at[s, :, n], e_sems.at[n])
            turned[s, n] = prod[s, x, (yh + k) % NYH] + xin[s, 0, n] + xin[s, 1, n] + xin[s, 2, n]
            if k:
                send(turned.at[s, n], yrecv.at[s, n], y_sems.at[s], 8, dyh=k)

    got((1, 0))
    pl.semaphore_wait(ready_x, 2)
    multiply(0)
    x_first(0)
    pl.semaphore_wait(far, 2)
    for d in (2, 1, 3):
        signal(cross, at(dx=d))
    for q in (0, 2, 1, 3):
        relay((0, 6), q, ((0, 5), up), ((1, 6), over))
        relay((0, 2), q, ((0, 3), down), ((1, 2), over))
        relay((1, 7), q, ((1, 5), dict(dz=2)))
        relay((1, 1), q, ((1, 3), dict(dz=6)))
    multiply(1)
    x_first(1)
    pl.semaphore_wait(cross, 3)
    for q in (0, 2, 1, 3):
        relay((0, 4), q, ((1, 4), over))
    got((1, 2), (1, 6), (0, 3))
    multiply(2)
    x_first(2)
    x_last(0)
    got((0, 5), (1, 4), (1, 5), (1, 3))
    multiply(3)
    x_first_short(3)
    batch = o % nbatch
    row_of = lax.broadcasted_iota(jnp.int32, (CAP, npt), 0)
    lane_of = lax.broadcasted_iota(jnp.int32, (CAP, npt), 1)
    weight = jnp.sum(
        jnp.where(lane_of == row_of + batch * CAP, w_ref[...], 0.0), axis=1, keepdims=True
    )
    count = jnp.sum(
        jnp.where(
            lax.broadcasted_iota(jnp.int32, (1, nbatch), 1) == batch,
            sz_ref[...].astype(jnp.float32), 0.0,
        ),
        axis=1, keepdims=True,
    )
    live = lax.broadcasted_iota(jnp.int32, (CAP, 1), 0).astype(jnp.float32) < count
    weight = jnp.where(live, weight, 0.0)
    x_last(1)
    x_last(2)
    x_last_short(3)

    lane = lax.broadcasted_iota(jnp.int32, (CAP, 2 * half), 1)
    units, rolled = [], []
    part = jnp.zeros((CAP, 1), jnp.float32)
    for s in range(4):
        unit = turned[s, yh] if s < 3 else turned[s, 2]
        if s < 3:
            arrive(yrecv.at[s], y_sems.at[s])
            unit = unit + yrecv[s, 0] + yrecv[s, 1] + yrecv[s, 2]
        else:
            arrive(oin, o_sems.at[0])
            unit = unit + oin[0] + oin[1] + oin[2] + oin[3]
            arrive(yrecv.at[s, pl.ds(0, 2)], y_sems.at[s])
            unit = unit + yrecv[s, 0] + yrecv[s, 1]
        other = pltpu.roll(unit, half, 1)
        units.append(unit)
        rolled.append(other)
        part += jnp.sum(jnp.where(lane < half, unit * other, 0.0), axis=1, keepdims=True)

    dens_out[...] = jnp.where(lane < half, part, weight)
    send(dens_out, dens_in, d_sems.at[0], 9, dc=1)
    arrive(dens_in, d_sems.at[0])
    total = 2 * nrow * NYL * NZ
    density = (part + dens_in[:, 0:1]) * (1.0 / math.sqrt(total))
    weight = jnp.where(o // nbatch == c, weight, dens_in[:, half : half + 1])
    for p in range(2):
        a, b = 2 * p, 2 * p + 1
        value = jnp.where(
            lane < half, density * units[a] + rolled[a], density * rolled[b] + units[b]
        )
        kall[p, o] = (weight * value).astype(jnp.bfloat16)

    def k_from(p, dx, dyh):
        return kall.at[p, occ_at(dx, dyh)]

    for p in (1, 0):
        for k in (2, 1, 3):
            send(k_from(p, 0, 0), k_from(p, 0, 0), k_sems.at[p, NYH - k], 10, dyh=k)
    for p in (1, 0):
        for k in (0, 1, 3, 2):
            if k:
                arrive(k_from(p, 0, k), k_sems.at[p, k])
            for d in (2, 1, 3):
                send(k_from(p, 0, k), k_from(p, 0, k), k_sems.at[p, 0], 10, dx=d)
    held = {}
    for p in (1, 0):
        arrive(kall.at[p, pl.ds(0, (NX - 1) * NYH)], k_sems.at[p, 0])
        kt = kall[p].reshape(2 * npt, 2 * half).T
        res = sum(
            jnp.dot(
                kt[:, k * npt : (k + 1) * npt], stran[k], preferred_element_type=jnp.float32
            )
            for k in range(NC)
        )
        slots = SETS[2 * p] + SETS[2 * p + 1]
        for dz in (4, 3, 5, 2, 6, 1, 7, 0):
            for dy in (1, 0):
                if (dy, dz) in slots:
                    i = slots.index((dy, dz))
                    block = res[i * nrow : (i + 1) * nrow]
                    if dy:
                        xsend[dz] = block.astype(jnp.bfloat16)
                        send(xsend.at[dz], xrecv.at[dz], d_sems.at[1 + dz], 11, dy=1)
                    else:
                        held[dz] = block
    mine = None
    for dz in (4, 3, 5, 2, 6, 1, 7, 0):
        arrive(xrecv.at[dz], d_sems.at[1 + dz])
        value = held[dz] + xrecv[dz].astype(jnp.float32)
        if dz:
            zsend[dz - 1] = value.astype(jnp.bfloat16)
            send(zsend.at[dz - 1], zrecv.at[dz - 1], d_sems.at[9], 12, dz=dz)
        else:
            mine = value
    for group, ref in enumerate((
        panels.at[pl.ds(0, 3)], panels.at[0, :, pl.ds(0, 3)], sigp, vraw, xin.at[pl.ds(0, 3)],
        yrecv.at[pl.ds(0, 3)], oin, xin.at[3, :, pl.ds(0, 3)], yrecv.at[3, pl.ds(0, 2)], dens_in,
        kall.at[:, pl.ds(0, 15)], xsend, zsend,
    )):
        all_sent(group, ref)
    arrive(zrecv, d_sems.at[9])
    for dz in range(1, NZ):
        mine = mine + zrecv[dz - 1].astype(jnp.float32)
    points = npt * NYL * NZ * NC
    out_ref[...] = mine[:, :m] * (1.0 / math.sqrt(points))


def per_device(orbital_values, occupied, trial, point_weights, batch_sizes, significant):
    v, occ, tri = orbital_values.T, occupied.T, trial.T
    m, npt = v.shape
    nrow = occ.shape[0]
    half = 4 * nrow
    wide = (m + 127) // 128 * 128
    f32, bf16 = jnp.float32, jnp.bfloat16
    dma = pltpu.SemaphoreType.DMA
    out = pl.pallas_call(
        kernel,
        out_shape=jax.ShapeDtypeStruct((nrow, m), f32),
        in_specs=[pl.BlockSpec(memory_space=pl.ANY)] * 6,
        out_specs=pl.BlockSpec(memory_space=pltpu.VMEM),
        scratch_shapes=[
            pltpu.VMEM((m, npt), bf16),
            pltpu.VMEM((1, npt), f32),
            pltpu.VMEM((1, batch_sizes.shape[0]), jnp.int32),
            pltpu.VMEM(significant.shape, jnp.int32),
            pltpu.VMEM((2, nrow, m), bf16),
            pltpu.VMEM((4, 2, 4, nrow, wide), bf16),
            pltpu.VMEM((m, npt), bf16),
            pltpu.VMEM(significant.shape, jnp.int32),
            pltpu.VMEM((NC, npt, wide), bf16),
            pltpu.VMEM((4, NX, NYH, CAP, 2 * half), f32),
        ]
        + [
            pltpu.VMEM((4, NX - 1, NYH, CAP, 2 * half), f32),
            pltpu.VMEM((NX, CAP, 2 * half), f32),
            pltpu.VMEM((4, NYH, CAP, 2 * half), f32),
            pltpu.VMEM((4, NYH - 1, CAP, 2 * half), f32),
            pltpu.VMEM((CAP, 2 * half), f32),
            pltpu.VMEM((CAP, 2 * half), f32),
            pltpu.VMEM((2, NX * NYH, CAP, 2 * half), bf16),
            pltpu.VMEM((NZ, nrow, wide), bf16),
            pltpu.VMEM((NZ, nrow, wide), bf16),
            pltpu.VMEM((NZ - 1, nrow, wide), bf16),
            pltpu.VMEM((NZ - 1, nrow, wide), bf16),
            dma((13,)),
            dma((28,)),
            dma((8,)),
            dma((2,)),
            dma((3,)),
            dma((3,)),
            dma((1,)),
            dma((4,)),
            dma((2, NYH)),
            dma((1 + 8 + 1,)),
            dma((6,)),
        ]
        + [pltpu.SemaphoreType.REGULAR] * 6,
        compiler_params=pltpu.CompilerParams(
            collective_id=0, has_side_effects=True, vmem_limit_bytes=24 << 20
        ),
    )(*(
        pltpu.with_memory_space_constraint(a, pltpu.HBM)
        for a in (v, occ, tri, point_weights.reshape(1, -1), batch_sizes.reshape(1, -1), significant)
    ))
    return out.T


def solution(mesh):
    placed = (
        P("grid", "occ"),
        P("occ", "grid"),
        P("occ", "grid"),
        P("grid"),
        P("grid"),
        P("grid", "occ"),
    )
    return jax.shard_map(
        per_device, mesh=mesh, in_specs=placed, out_specs=P("occ", "grid"), check_vma=False
    )
```
